32 devices in a mesh: groups: 2 (over x), pts: 8 (over z, y), sn: 2 (over core).
Axes of the slice: x: 2, y: 2, z: 4, core: 2. Of those that a mesh axis runs over, the one named last changes fastest.
Arguments:
- point_features: bfloat16 [131072, 192], P(('groups', 'pts', 'sn')), parts along dimension 0, may hold values from -6 to 6
- point_positions: float32 [3, 131072], P(None, ('groups', 'pts', 'sn')), parts along dimension 1, may hold values from 0 to 1
- sn_positions: float32 [3, 32768], P(None, ('groups', 'pts', 'sn')), parts along dimension 1, may hold values from 0 to 1
- latent_queries: bfloat16 [512, 192], replicated, may hold values from -500 to 500
- target_block: int32 [256], P('groups'), parts along dimension 0, may hold values from 0 to 127, as said below
- target_links: int32 [256, 3], P(('groups', 'pts', 'sn')), parts along dimension 0, may hold values from 0 to 31
- target_count: int32 [32], P('groups'), parts along dimension 0, may hold values from 6 to 8, as said below
- block_slot: int32 [256], P('groups'), parts along dimension 0, may hold values from 0 to 127, as said below
- w_in: bfloat16 [192, 192], replicated, may hold values from -0.4375 to 0.4375
- w_mid: bfloat16 [192, 192], replicated, may hold values from -0.4375 to 0.4375
- w_post: bfloat16 [192, 192], replicated, may hold values from -1.25 to 1.25
- w_key: bfloat16 [192, 192], replicated, may hold values from -0.4375 to 0.4375
- w_value: bfloat16 [192, 192], replicated, may hold values from -0.4375 to 0.4375
- w_out: bfloat16 [192, 192], replicated, may hold values from -0.4375 to 0.4375
- out_gain: float32 [192], replicated, may hold values from 0.1 to 1.9
Outputs:
- supernode_features: bfloat16 [32768, 192], P(('groups', 'pts', 'sn')), parts along dimension 0
- latent_out: bfloat16 [1024, 192], P(('groups', 'pts', 'sn')), parts along dimension 0
The draws below stay inside these ranges and needn't reach their ends.
There are 2 independent parts, one for each index of `groups`. The reference program is written for one: setup_inputs(seed, part) draws one part's arguments, and reference() takes and returns one part's arrays. A program takes and returns all parts, laid end to end along the dimension named above; an argument that names none is the same for every part. Nothing has to cross between parts.
Inputs may be any that keep to these rules, and one draw needn't show every extreme that they name: `target_block`: the 8 targets of one region name blocks of distinct owners, the owner of a block being its slot divided by 8; one owner, the same for all regions, holds the first target of every region. `target_count`: the live targets of a region are its first ones; some region has all 8 live. `block_slot`: A permutation.
All inputs are finite; a program needn't handle non-finite values.
Results may differ from the reference program's by a relative error of at most 0.012.
The reference program's roundings to bfloat16 on the way count: a program that leaves them out, or rounds other values in their place, can miss the bound.
Values may be sent and summed in bfloat16 or wider, within the bound.
A program may use at most 256 MiB of HBM per device.

```python
import jax
import jax.numpy as jnp
from jax import lax

D = 192
HEADS = 3
BLOCK = 128
LINKS = 3
PB_DEV = 32
SNB_DEV = 8
LATENTS = 512
KEY_BLOCK = 512
OWNERS = 16
TARGETS_DEV = 8
SN_BLOCKS = 128
SUPERNODES = 16384
POINTS = 65536
N_PTS = 8
N_SN = 2


def graph_tables(key):
    slot_of_block = jax.random.permutation(jax.random.fold_in(key, 11), SN_BLOCKS).astype(jnp.int32)
    block_of_slot = jnp.zeros((SN_BLOCKS,), jnp.int32).at[slot_of_block].set(jnp.arange(SN_BLOCKS, dtype=jnp.int32))
    hot_owner = jax.random.randint(jax.random.fold_in(key, 12), (), 0, OWNERS)
    row_keys = jax.random.split(jax.random.fold_in(key, 13), OWNERS)
    others = jax.vmap(lambda one_key: jax.random.permutation(one_key, OWNERS - 1))(row_keys)[:, :TARGETS_DEV - 1]
    owner_rows = jnp.concatenate([jnp.full((OWNERS, 1), hot_owner, jnp.int32), ((hot_owner + 1 + others) % OWNERS).astype(jnp.int32)], axis=1)
    local_rows = jax.random.randint(jax.random.fold_in(key, 14), (OWNERS, TARGETS_DEV), 0, SNB_DEV)
    targets = block_of_slot[owner_rows * SNB_DEV + local_rows]
    counts = jax.random.randint(jax.random.fold_in(key, 15), (OWNERS,), TARGETS_DEV * 3 // 4, TARGETS_DEV + 1)
    full_region = jax.random.randint(jax.random.fold_in(key, 16), (), 0, OWNERS)
    counts = counts.at[full_region].set(TARGETS_DEV)
    return (slot_of_block, targets.reshape(-1).astype(jnp.int32), counts.astype(jnp.int32))


def draw_block_slot(key, part):
    return graph_tables(key)[0]


def draw_target_block(key, part):
    return graph_tables(key)[1]


def draw_target_count(key, part):
    return graph_tables(key)[2]


def draw_latent_queries(key, part):
    base = jax.random.truncated_normal(key, -4.0, 4.0, (LATENTS, D), jnp.float32)
    return base.astype(jnp.bfloat16)


def with_ends(drawn, stream_key, low, top_value):
    longest = drawn.shape.index(max(drawn.shape))
    spots = []
    for shift in (0, 1):
        where = [jax.random.randint(jax.random.fold_in(stream_key, axis), (), 0, length) for axis, length in enumerate(drawn.shape)]
        where[longest] = (where[longest] + shift) % drawn.shape[longest]
        spots.append(tuple(where))
    return drawn.at[spots[0]].set(low).at[spots[1]].set(top_value)


def shard_levels(stream_key, dims, cuts, smallest, top_value):
    def one(axis_at, shards_of):
        steps = jax.random.uniform(jax.random.fold_in(jax.random.fold_in(stream_key, 6), axis_at), (shards_of,), jnp.float32, smallest / len(cuts), top_value / len(cuts))
        return jnp.repeat(jnp.exp(steps), dims[axis_at] // shards_of).reshape((-1,) + (1,) * (len(dims) - axis_at - 1))

    gain = one(*cuts[0])
    for cut in cuts[1:]:
        gain = gain * one(*cut)
    return gain


def noise(stream_key, shape, spread, limit, cuts=(), kind=jnp.bfloat16):
    values = jax.random.normal(stream_key, shape, jnp.float32) * spread
    if len(cuts) > 0:
        values = shard_levels(stream_key, shape, cuts, -0.22, 0.18) * values
    return jnp.clip(values, min=-limit, max=limit).astype(kind)


def setup_inputs(seed: int = 0, part: int = 0) -> dict:
    seeds = jax.random.split(jax.random.key(seed), 16)
    part_splits = jax.random.split(jax.random.fold_in(seeds[15], part), 16)
    point_features = noise(part_splits[0], (POINTS, D), 1.0, 6.0, ((0, 16),))
    point_positions = jnp.clip(1.0 * jax.random.uniform(part_splits[1], (3, POINTS), jnp.float32) ** shard_levels(part_splits[1], (3, POINTS), ((1, 16),), -0.2, 0.2), 0.0, 1.0)
    sn_positions = jnp.clip(1.0 * jax.random.uniform(part_splits[2], (3, SUPERNODES), jnp.float32) ** shard_levels(part_splits[2], (3, SUPERNODES), ((1, 16),), -0.2, 0.2), 0.0, 1.0)
    latent_queries = draw_latent_queries(jax.random.fold_in(seeds[15], 71), part)
    target_block = draw_target_block(jax.random.fold_in(jax.random.fold_in(seeds[15], part), 71), part)
    target_links = with_ends(jax.random.randint(part_splits[5], (OWNERS * TARGETS_DEV, LINKS), 0, PB_DEV), jax.random.fold_in(part_splits[5], 1), 0, PB_DEV - 1).astype(jnp.int32)
    target_count = draw_target_count(jax.random.fold_in(jax.random.fold_in(seeds[15], part), 71), part)
    block_slot = draw_block_slot(jax.random.fold_in(jax.random.fold_in(seeds[15], part), 71), part)
    w_in = noise(seeds[8], (D, D), D ** -0.5, 0.4375)
    w_mid = noise(seeds[9], (D, D), D ** -0.5, 0.4375)
    w_post = noise(seeds[10], (D, D), (D // 8) ** -0.5, 1.25)
    w_key = noise(seeds[11], (D, D), D ** -0.5, 0.4375)
    w_value = noise(seeds[12], (D, D), D ** -0.5, 0.4375)
    w_out = noise(seeds[13], (D, D), D ** -0.5, 0.4375)
    out_gain = jnp.clip(1.0 + 0.18 * jax.random.normal(seeds[14], (D,), jnp.float32), 0.1, 1.9)
    return {"point_features": point_features, "point_positions": point_positions, "sn_positions": sn_positions, "latent_queries": latent_queries, "target_block": target_block, "target_links": target_links, "target_count": target_count, "block_slot": block_slot, "w_in": w_in, "w_mid": w_mid, "w_post": w_post, "w_key": w_key, "w_value": w_value, "w_out": w_out, "out_gain": out_gain}


INV_RADIUS_SQ = 100.0

def combine_parts(first, second):
    peak_a, total_a, output_a = first
    peak_b, total_b, output_b = second
    peak = jnp.maximum(peak_a, peak_b)
    scale_a = jnp.exp(peak_a - peak)
    scale_b = jnp.exp(peak_b - peak)
    total = total_a * scale_a + total_b * scale_b
    rows = output_a.shape[0]
    heads = peak.shape[-1]
    output = output_a.reshape(rows, heads, -1) * scale_a[..., None] + output_b.reshape(rows, heads, -1) * scale_b[..., None]
    return (peak, total, output.reshape(rows, -1))

def block_attend(queries, keys_blk, values_blk):
    rows, width = queries.shape
    head_width = width // HEADS
    query_heads = queries.astype(jnp.float32).reshape(rows, HEADS, head_width)
    key_heads = keys_blk.astype(jnp.float32).reshape(-1, HEADS, head_width)
    value_heads = values_blk.astype(jnp.float32).reshape(-1, HEADS, head_width)
    scores = jnp.einsum('lhd,khd->lhk', query_heads, key_heads) * head_width ** (-0.5)
    peak = lax.optimization_barrier(jnp.max(scores, axis=-1))
    weights = jnp.exp(scores - peak[..., None])
    total = lax.optimization_barrier(jnp.sum(weights, axis=-1))
    rounded = lax.optimization_barrier(weights.astype(jnp.bfloat16)).astype(jnp.float32)
    output = jnp.einsum('lhk,khd->lhd', rounded, value_heads).reshape(rows, width)
    return (peak, total, output)

def reference(point_features, point_positions, sn_positions, latent_queries, target_block, target_links, target_count, block_slot, w_in, w_mid, w_post, w_key, w_value, w_out, out_gain):
    owners = N_PTS * N_SN
    width = point_features.shape[1]
    slot_table = block_slot[target_block].reshape(owners, TARGETS_DEV)
    live_table = jnp.arange(TARGETS_DEV)[None, :] < target_count[:, None]
    sn_blocks_all = sn_positions.reshape(3, SN_BLOCKS, BLOCK)
    region_feats = point_features.reshape(owners, PB_DEV * BLOCK, width)
    region_pos = jnp.transpose(point_positions.reshape(3, owners, PB_DEV, BLOCK), (1, 0, 2, 3))
    region_links = target_links.reshape(owners, TARGETS_DEV, LINKS)

    def per_region(carry, region):
        gathered, weight_sum = carry
        feats, positions, link_rows, slot_row, live_row = region
        inner_act = jax.nn.gelu(jnp.dot(feats, w_in, preferred_element_type=jnp.float32)).astype(jnp.bfloat16)
        hidden = jnp.dot(inner_act, w_mid, preferred_element_type=jnp.float32).astype(jnp.bfloat16)
        hidden_blocks = hidden.reshape(PB_DEV, BLOCK, width)
        target_pos = sn_blocks_all[:, slot_row]
        linked_pos = positions[:, link_rows]
        gaps = target_pos[:, :, None, :, None] - linked_pos[:, :, :, None, :]
        kernel = 1.0 / (1.0 + lax.optimization_barrier(jnp.sum(gaps * gaps, axis=0)) * INV_RADIUS_SQ)
        totals = lax.optimization_barrier(jnp.sum(kernel, axis=(1, 3)))
        rounded = lax.optimization_barrier(kernel.astype(jnp.bfloat16)).astype(jnp.float32)
        sums = jnp.einsum('tlji,tlic->tjc', rounded, hidden_blocks[link_rows].astype(jnp.float32))
        sums = jnp.where(live_row[:, None, None], sums, 0.0).astype(jnp.bfloat16)
        totals = jnp.where(live_row[:, None], totals, 0.0).astype(jnp.bfloat16)
        sums = lax.optimization_barrier(sums).astype(jnp.float32)
        totals = lax.optimization_barrier(totals).astype(jnp.float32)
        gathered = gathered.at[slot_row].add(sums)
        weight_sum = weight_sum.at[slot_row].add(totals)
        return ((gathered, weight_sum), None)
    start = (jnp.zeros((SN_BLOCKS, BLOCK, width), jnp.float32), jnp.zeros((SN_BLOCKS, BLOCK), jnp.float32))
    (gathered, weight_sum), unused = lax.scan(per_region, start, (region_feats, region_pos, region_links, slot_table, live_table))
    pooled = (gathered / (1.0 + weight_sum[..., None])).astype(jnp.bfloat16).reshape(SUPERNODES, width)
    supernode_features = jax.nn.gelu(jnp.dot(pooled, w_post, preferred_element_type=jnp.float32)).astype(jnp.bfloat16)
    keys = jnp.dot(supernode_features, w_key, preferred_element_type=jnp.float32).astype(jnp.bfloat16)
    values = jnp.dot(supernode_features, w_value, preferred_element_type=jnp.float32).astype(jnp.bfloat16)
    rows = latent_queries.shape[0]
    init = (jnp.full((rows, HEADS), -jnp.inf, jnp.float32), jnp.zeros((rows, HEADS), jnp.float32), jnp.zeros((rows, width), jnp.float32))

    def key_step(carry, block_inputs):
        return (combine_parts(carry, block_attend(latent_queries, block_inputs[0], block_inputs[1])), None)
    partial_state, unused = lax.scan(key_step, init, (keys.reshape(-1, KEY_BLOCK, width), values.reshape(-1, KEY_BLOCK, width)))
    peak, total, output = partial_state
    attended = (output.reshape(rows, HEADS, -1) / total[..., None]).reshape(rows, width).astype(jnp.bfloat16)
    projected = jnp.dot(attended, w_out, preferred_element_type=jnp.float32)
    mean_sq = lax.optimization_barrier(jnp.mean(projected * projected, axis=-1, keepdims=True))
    latent_out = (projected * lax.rsqrt(mean_sq + 1e-06) * out_gain.astype(jnp.float32)).astype(jnp.bfloat16)
    return (supernode_features, latent_out)
```

```python
import functools

import jax
import jax.numpy as jnp
from jax import lax
from jax.experimental import pallas as pl
from jax.experimental.pallas import tpu as pltpu
from jax.sharding import PartitionSpec as P

HEADS = 3
BLOCK = 128
INV_RADIUS_SQ = 100.0
MESH = pl.DeviceIdType.MESH
STAT_ROWS = 8
CHUNK = 1024
LATENT_CHUNK = 256
OUT_LANES = 256
VMEM_LIMIT = 28 * 2**20
F32 = jnp.float32
BF16 = jnp.bfloat16


def contract(a, b, dim_a, dim_b):
    return lax.dot_general(a, b, (((dim_a,), (dim_b,)), ((), ())), preferred_element_type=F32)


def place(n_sn):
    return lax.axis_index("pts") * n_sn + lax.axis_index("sn")


def peer(index, n_sn):
    return {"pts": lax.div(index, n_sn), "sn": lax.rem(index, n_sn)}


def greet(owners, me, n_sn):
    barrier = pltpu.get_barrier_semaphore()

    def signal(off, carry):
        other = lax.rem(me + off, owners)
        pl.semaphore_signal(barrier, inc=1, device_id=peer(other, n_sn), device_id_type=MESH)
        return carry

    lax.fori_loop(1, owners, signal, 0)
    return barrier


def far_first(i, owners):
    return owners // 2 + lax.div(i + 1, 2) * (2 * lax.rem(i + 1, 2) - 1)


def named_block(owner, targets, sn_blocks, count, slot_at):
    def look(k, state):
        which, block, live = state
        slot = slot_at(k)
        hit = jnp.logical_and(lax.div(slot, sn_blocks) == owner, k < count)
        return (
            jnp.where(hit, k, which),
            jnp.where(hit, lax.rem(slot, sn_blocks), block),
            jnp.where(hit, 1.0, live),
        )

    start = (jnp.int32(0), jnp.int32(0), F32(0.0))
    return lax.fori_loop(0, targets, look, start, unroll=targets <= 8)


def columns_of(rows):
    padded = jnp.concatenate([rows, jnp.zeros((5, rows.shape[1]), F32)], axis=0)
    return jnp.transpose(padded)


def thirds(x):
    first = x.astype(BF16).astype(F32)
    second = (x - first).astype(BF16).astype(F32)
    third = x - first - second
    return [first, second, third]


def encoder_kernel(
    owners,
    n_sn,
    sn_blocks,
    targets,
    target_block_in,
    target_links_in,
    target_count_in,
    block_slot_in,
    feats_in,
    positions_in,
    sn_positions_in,
    w_in_in,
    w_mid_in,
    w_post_in,
    queries_in,
    w_key_in,
    w_value_in,
    features_out,
    landed,
    target_block,
    target_links,
    target_count,
    block_slot,
    points,
    positions,
    sn_positions,
    w_in,
    w_mid,
    w_post,
    queries,
    w_key,
    w_value,
    features,
    load_sem,
    pooled,
    values_t,
    keys,
    parts,
    part_send,
    part_recv,
    arrived,
    sums,
    block_of,
    wanted,
    everywhere,
    hidden,
    point_blocks,
    outgoing,
    slots,
    pos_send,
    pos_recv,
    msg_send,
    msg_recv,
    own_sem,
):
    me = place(n_sn)
    links = target_links.shape[0]
    width = points.shape[0]
    loads = [
        pltpu.make_async_copy(source, target, load_sem.at[i])
        for i, (source, target) in enumerate(
            [
                (target_block_in, target_block),
                (block_slot_in, block_slot),
                (target_count_in, target_count),
                (target_links_in, target_links),
                (sn_positions_in, sn_positions),
                (feats_in, points),
                (w_in_in, w_in),
                (w_mid_in, w_mid),
                (positions_in, positions),
                (w_post_in, w_post),
                (w_key_in, w_key),
                (w_value_in, w_value),
                (queries_in, queries),
            ]
        )
    ]
    for load in loads[:5]:
        load.start()
    barrier = greet(owners, me, n_sn)
    for load in loads[5:]:
        load.start()
    for load in loads[:5]:
        load.wait()

    def choose(region, carry):
        def slot_at(k):
            return block_slot[target_block[region * targets + k]]

        block = named_block(me, targets, sn_blocks, target_count[region], slot_at)[1]
        block_of[region] = block
        rows = sn_positions[:, :BLOCK]
        for b in range(1, sn_blocks):
            rows = jnp.where(block == b, sn_positions[:, b * BLOCK : (b + 1) * BLOCK], rows)
        wanted[region] = rows
        return carry

    lax.fori_loop(0, owners, choose, 0)

    def slot_of(k, carry):
        slots[k] = block_slot[target_block[me * targets + k]]
        return carry

    lax.fori_loop(0, targets, slot_of, 0)
    my_count = target_count[me]

    def pos_copy(other, slot_at):
        return pltpu.make_async_remote_copy(
            src_ref=wanted.at[other],
            dst_ref=everywhere.at[slot_at],
            send_sem=pos_send.at[other],
            recv_sem=pos_recv.at[slot_at],
            device_id=peer(other, n_sn),
            device_id_type=MESH,
        )

    def start_pos(i, carry):
        pos_copy(lax.rem(me + far_first(i, owners), owners), me).start()
        return carry

    def mlp(step, carry):
        span = pl.ds(pl.multiple_of(step * CHUNK, CHUNK), CHUNK)
        inner = jax.nn.gelu(contract(w_in[...], points[:, span], 0, 0)).astype(BF16)
        hid = contract(w_mid[...], inner, 0, 0).astype(BF16)
        places = positions[:, span]
        for q in range(CHUNK // BLOCK):
            hidden[step * (CHUNK // BLOCK) + q] = hid[:, q * BLOCK : (q + 1) * BLOCK]
            point_blocks[step * (CHUNK // BLOCK) + q] = places[:, q * BLOCK : (q + 1) * BLOCK]
        return carry

    mlp_steps = points.shape[1] // CHUNK
    for load in loads[5:9]:
        load.wait()
    lax.fori_loop(0, mlp_steps // 2, mlp, 0)
    pl.semaphore_wait(barrier, owners - 1)
    lax.fori_loop(0, owners - 1, start_pos, 0)
    own_pos = pltpu.make_async_copy(wanted.at[me], everywhere.at[me], own_sem.at[0])
    own_pos.start()
    lax.fori_loop(mlp_steps // 2, mlp_steps, mlp, 0)
    for load in loads[9:]:
        load.wait()

    def msg_copy(other, slot_at):
        return pltpu.make_async_remote_copy(
            src_ref=outgoing.at[other],
            dst_ref=arrived.at[slot_at],
            send_sem=msg_send.at[other],
            recv_sem=msg_recv.at[slot_at],
            device_id=peer(other, n_sn),
            device_id_type=MESH,
        )

    def build(other):
        which, block, live = named_block(
            other, targets, sn_blocks, my_count, lambda k: slots[k]
        )
        sn_cols = columns_of(everywhere[other])
        kernels = []
        blocks = []
        for j in range(links):
            link = target_links[j, which]
            pts = point_blocks[link]
            dist = jnp.zeros((BLOCK, BLOCK), F32)
            for c in range(3):
                gap = sn_cols[:, c : c + 1] - pts[c : c + 1, :]
                dist = dist + gap * gap
            kernels.append(1.0 / (1.0 + dist * INV_RADIUS_SQ))
            blocks.append(hidden[link])
        total = kernels[0]
        for extra in kernels[1:]:
            total = total + extra
        total = jnp.sum(jnp.transpose(total), axis=0, keepdims=True)
        message = contract(
            jnp.concatenate(blocks, axis=1),
            jnp.concatenate([one.astype(BF16) for one in kernels], axis=1),
            1,
            1,
        )
        outgoing[other, :width, :] = (message * live).astype(BF16)
        outgoing[other, width:, :] = jnp.broadcast_to(total * live, (STAT_ROWS, BLOCK)).astype(BF16)

    def nth(i):
        return lax.rem(me + far_first(i, owners), owners)

    def build_next(i):
        pos_copy(nth(i), nth(i)).wait_recv()
        build(nth(i))

    build_next(0)

    def send(i, carry):
        build_next(i)
        msg_copy(nth(i - 1), me).start()
        return carry

    lax.fori_loop(1, owners - 1, send, 0)
    own_pos.wait()
    build(me)
    msg_copy(nth(owners - 2), me).start()
    def add(source, message):
        block = block_of[source]
        for b in range(sn_blocks):
            sums[b] += jnp.where(block == b, message, 0.0)

    sums[...] = jnp.zeros_like(sums)
    add(me, outgoing[me].astype(F32))

    def finish(i, carry):
        source = nth(lax.rem(i + owners // 2 + 1, owners - 1))
        msg_copy(source, source).wait_recv()
        add(source, arrived[source].astype(F32))
        return carry

    lax.fori_loop(0, owners - 1, finish, 0)

    def sent(i, carry):
        msg_copy(nth(i), nth(i)).wait_send()
        pos_copy(nth(i), nth(i)).wait_send()
        return carry

    lax.fori_loop(0, owners - 1, sent, 0)
    for b in range(sn_blocks):
        scale = 1.0 / (1.0 + sums[b, width : width + 1, :])
        pooled[:, b * BLOCK : (b + 1) * BLOCK] = (sums[b, :width, :] * scale).astype(BF16)


    head_width = width // HEADS
    latents = queries.shape[1]
    share = latents // owners
    chunks = latents // LATENT_CHUNK
    per_chunk = LATENT_CHUNK // share
    features[...] = jax.nn.gelu(contract(w_post[...], pooled[...], 0, 0)).astype(BF16)
    store = pltpu.make_async_copy(features, features_out, own_sem.at[2])
    store.start()
    keys[...] = contract(features[...], w_key[...], 0, 0).astype(BF16)
    values_t[...] = contract(w_value[...], features[...], 0, 0).astype(BF16)
    row_head = lax.broadcasted_iota(jnp.int32, (width, LATENT_CHUNK), 0) // head_width
    first = lax.div(me, per_chunk) + chunks // 2

    def attend(step, carry):
        chunk = lax.rem(first + step, chunks)
        at = pl.multiple_of(chunk * LATENT_CHUNK, LATENT_CHUNK)
        part = queries[:, pl.ds(at, LATENT_CHUNK)] * BF16(head_width ** (-0.5))
        outs, peaks, totals = [], [], []
        for h in range(HEADS):
            scores = contract(keys[...], jnp.where(row_head == h, part, BF16(0.0)), 1, 0)
            peak = jnp.max(scores, axis=0, keepdims=True)
            probs = jnp.exp(scores - peak)
            totals += thirds(jnp.sum(probs, axis=0, keepdims=True))
            peaks += thirds(peak)
            own_values = values_t[h * head_width : (h + 1) * head_width, :]
            outs.append(contract(own_values, probs.astype(BF16), 1, 0))
        pad = jnp.zeros((OUT_LANES - width - 6 * HEADS, LATENT_CHUNK), F32)
        whole = jnp.transpose(jnp.concatenate(outs + peaks + totals + [pad], axis=0))
        for j in range(per_chunk):
            parts[chunk * per_chunk + j] = whole[j * share : (j + 1) * share, :].astype(BF16)
        return carry

    def copy_of(other, slot_at):
        return pltpu.make_async_remote_copy(
            src_ref=parts.at[other],
            dst_ref=landed.at[slot_at],
            send_sem=part_send.at[other],
            recv_sem=part_recv.at[slot_at],
            device_id=peer(other, n_sn),
            device_id_type=MESH,
        )

    def send_chunk(step):
        chunk = lax.rem(first + step, chunks)

        def start(j, carry):
            other = chunk * per_chunk + lax.rem(me + j, per_chunk)

            @pl.when(other != me)
            def _():
                copy_of(other, me).start()

            return carry

        lax.fori_loop(0, per_chunk, start, 0)

    attend(0, 0)

    def step_on(step, carry):
        send_chunk(step - 1)
        return attend(step, carry)

    lax.fori_loop(1, chunks, step_on, 0)
    send_chunk(chunks - 1)
    own = pltpu.make_async_copy(parts.at[me], landed.at[me], own_sem.at[1])
    own.start()
    own.wait()

    def settle(off, carry):
        other = lax.rem(me + off, owners)
        copy = copy_of(other, other)
        copy.wait_send()
        copy.wait_recv()
        return carry

    lax.fori_loop(1, owners, settle, 0)
    store.wait()


def finish_kernel(features_in, landed, w_out, out_gain, features, latent_out, sem):
    move = pltpu.make_async_copy(features_in, features, sem)
    move.start()
    owners, share, _ = landed.shape
    width = w_out.shape[0]
    head_width = width // HEADS
    lane = lax.broadcasted_iota(jnp.int32, (OUT_LANES, width), 0) - width
    head_of = lax.broadcasted_iota(jnp.int32, (OUT_LANES, width), 1) // head_width
    is_peak = jnp.logical_and(lane >= 3 * head_of, lane < 3 * head_of + 3)
    total_lane = lane - 3 * HEADS
    is_total = jnp.logical_and(total_lane >= 3 * head_of, total_lane < 3 * head_of + 3)
    flat = jnp.concatenate([landed[source] for source in range(owners)], axis=0)
    peaks = contract(flat, jnp.where(is_peak, 1.0, 0.0).astype(BF16), 1, 0)
    totals = contract(flat, jnp.where(is_total, 1.0, 0.0).astype(BF16), 1, 0)

    def of(full, source):
        return full[source * share : (source + 1) * share, :]

    top = of(peaks, 0)
    for source in range(1, owners):
        top = jnp.maximum(top, of(peaks, source))
    output = jnp.zeros((share, width), F32)
    total = jnp.zeros((share, width), F32)
    for source in range(owners):
        scale = jnp.exp(of(peaks, source) - top)
        output = output + scale * landed[source][:, :width].astype(F32)
        total = total + scale * of(totals, source)
    attended = (output / total).astype(BF16)
    projected = jnp.dot(attended, w_out[...], preferred_element_type=F32)
    mean_sq = jnp.mean(projected * projected, axis=-1, keepdims=True)
    normed = projected * lax.rsqrt(mean_sq + 1e-06)
    latent_out[...] = (normed * out_gain[...]).astype(BF16)
    move.wait()


def per_device(
    n_sn,
    owners,
    point_features,
    point_positions,
    sn_positions,
    latent_queries,
    target_block,
    target_links,
    target_count,
    block_slot,
    w_in,
    w_mid,
    w_post,
    w_key,
    w_value,
    w_out,
    out_gain,
):
    targets = target_links.shape[0]
    width = point_features.shape[1]
    sn_rows = sn_positions.shape[1]
    sn_blocks = sn_rows // BLOCK
    latents = latent_queries.shape[0]
    share = latents // owners
    vmem = pl.BlockSpec(memory_space=pltpu.VMEM)
    hbm = pl.BlockSpec(memory_space=pl.ANY)
    dma = pltpu.SemaphoreType.DMA
    points = point_features.shape[0]
    features_t, landed = pl.pallas_call(
        functools.partial(encoder_kernel, owners, n_sn, sn_blocks, targets),
        out_shape=(
            jax.ShapeDtypeStruct((width, sn_rows), BF16),
            jax.ShapeDtypeStruct((owners, share, OUT_LANES), BF16),
        ),
        in_specs=[hbm] * 13,
        out_specs=(hbm, hbm),
        scratch_shapes=[
            pltpu.SMEM(target_block.shape, jnp.int32),
            pltpu.SMEM(target_links.shape[::-1], jnp.int32),
            pltpu.SMEM(target_count.shape, jnp.int32),
            pltpu.SMEM(block_slot.shape, jnp.int32),
            pltpu.VMEM((width, points), BF16),
            pltpu.VMEM(point_positions.shape, F32),
            pltpu.VMEM(sn_positions.shape, F32),
            pltpu.VMEM(w_in.shape, BF16),
            pltpu.VMEM(w_mid.shape, BF16),
            pltpu.VMEM(w_post.shape, BF16),
            pltpu.VMEM(latent_queries.shape[::-1], BF16),
            pltpu.VMEM(w_key.shape, BF16),
            pltpu.VMEM(w_value.shape, BF16),
            pltpu.VMEM((width, sn_rows), BF16),
            dma((13,)),
            pltpu.VMEM((width, sn_rows), BF16),
            pltpu.VMEM((width, sn_rows), BF16),
            pltpu.VMEM((sn_rows, width), BF16),
            pltpu.VMEM((owners, share, OUT_LANES), BF16),
            dma((owners,)),
            dma((owners,)),
            pltpu.VMEM((owners, width + STAT_ROWS, BLOCK), BF16),
            pltpu.VMEM((sn_blocks, width + STAT_ROWS, BLOCK), F32),
            pltpu.SMEM((owners,), jnp.int32),
            pltpu.VMEM((owners, 3, BLOCK), F32),
            pltpu.VMEM((owners, 3, BLOCK), F32),
            pltpu.VMEM((points // BLOCK, width, BLOCK), BF16),
            pltpu.VMEM((points // BLOCK, 3, BLOCK), F32),
            pltpu.VMEM((owners, width + STAT_ROWS, BLOCK), BF16),
            pltpu.SMEM((targets,), jnp.int32),
            dma((owners,)),
            dma((owners,)),
            dma((owners,)),
            dma((owners,)),
            dma((3,)),
        ],
        compiler_params=pltpu.CompilerParams(
            collective_id=0, has_side_effects=True, vmem_limit_bytes=VMEM_LIMIT
        ),
        name="encoder",
    )(
        *(
            pltpu.with_memory_space_constraint(operand, pltpu.HBM)
            for operand in (
                target_block,
                target_links.T,
                target_count,
                block_slot,
                point_features.T,
                point_positions,
                sn_positions,
                w_in,
                w_mid,
                w_post,
                latent_queries.T,
                w_key,
                w_value,
            )
        )
    )
    features_t, latent_out = pl.pallas_call(
        finish_kernel,
        out_shape=(
            jax.ShapeDtypeStruct((width, sn_rows), BF16),
            jax.ShapeDtypeStruct((share, width), BF16),
        ),
        in_specs=[hbm] + [vmem] * 3,
        out_specs=(hbm, vmem),
        scratch_shapes=[dma],
        compiler_params=pltpu.CompilerParams(vmem_limit_bytes=VMEM_LIMIT),
        name="finish",
    )(features_t, landed, w_out, out_gain.reshape(1, width))
    return (features_t.T, latent_out)


def solution(mesh):
    n_sn = mesh.shape["sn"]
    owners = mesh.shape["pts"] * n_sn
    everything = ("groups", "pts", "sn")
    in_specs = (
        P(everything, None),
        P(None, everything),
        P(None, everything),
        P(),
        P("groups"),
        P(everything, None),
        P("groups"),
        P("groups"),
        P(),
        P(),
        P(),
        P(),
        P(),
        P(),
        P(),
    )
    out_specs = (P(everything, None), P(everything, None))
    return jax.shard_map(
        functools.partial(per_device, n_sn, owners),
        mesh=mesh,
        in_specs=in_specs,
        out_specs=out_specs,
        check_vma=False,
    )
```

```python
import functools

import jax
import jax.numpy as jnp
from jax import lax
from jax.experimental import pallas as pl
from jax.experimental.pallas import tpu as pltpu
from jax.sharding import PartitionSpec as P

HEADS = 3
BLOCK = 128
INV_RADIUS_SQ = 100.0
MESH = pl.DeviceIdType.MESH
STAT_ROWS = 8
CHUNK = 1024
LATENT_CHUNK = 256
OUT_LANES = 256
VMEM_LIMIT = 40 * 2**20
F32 = jnp.float32
BF16 = jnp.bfloat16


def contract(a, b, dim_a, dim_b):
    return lax.dot_general(a, b, (((dim_a,), (dim_b,)), ((), ())), preferred_element_type=F32)


def place(n_sn):
    return lax.axis_index("pts") * n_sn + lax.axis_index("sn")


def peer(index, n_sn):
    return {"pts": lax.div(index, n_sn), "sn": lax.rem(index, n_sn)}


def greet(owners, me, n_sn):
    barrier = pltpu.get_barrier_semaphore()

    def signal(off, carry):
        other = lax.rem(me + off, owners)
        pl.semaphore_signal(barrier, inc=1, device_id=peer(other, n_sn), device_id_type=MESH)
        return carry

    lax.fori_loop(1, owners, signal, 0)
    return barrier


def early_steps(steps):
    left = 3 - lax.div(lax.axis_index("pts") * 4, lax.axis_size("pts"))
    return steps // 2 * lax.div(left * left, 4)


def far_first(i, owners):
    return owners // 2 + lax.div(i + 1, 2) * (2 * lax.rem(i + 1, 2) - 1)


def named_block(owner, targets, sn_blocks, count, slot_at):
    def look(k, state):
        which, block, live = state
        slot = slot_at(k)
        hit = jnp.logical_and(lax.div(slot, sn_blocks) == owner, k < count)
        return (
            jnp.where(hit, k, which),
            jnp.where(hit, lax.rem(slot, sn_blocks), block),
            jnp.where(hit, 1.0, live),
        )

    start = (jnp.int32(0), jnp.int32(0), F32(0.0))
    return lax.fori_loop(0, targets, look, start, unroll=targets <= 8)


def low_lanes(shape):
    return lax.broadcasted_iota(jnp.int32, shape, 1) < BLOCK // 2


def swap_halves(upper, lower):
    low = low_lanes(upper.shape)
    half = BLOCK // 2
    return (
        jnp.where(low, upper, pltpu.roll(lower, half, 1)),
        jnp.where(low, pltpu.roll(upper, half, 1), lower),
    )


def columns_of(rows):
    padded = jnp.concatenate([rows, jnp.zeros((5, rows.shape[1]), F32)], axis=0)
    return jnp.transpose(padded)


def thirds(x):
    first = x.astype(BF16).astype(F32)
    second = (x - first).astype(BF16).astype(F32)
    third = x - first - second
    return [first, second, third]


def encoder_kernel(
    owners,
    n_sn,
    sn_blocks,
    targets,
    target_block_in,
    target_links_in,
    target_count_in,
    block_slot_in,
    feats_in,
    positions_in,
    sn_positions_in,
    w_in_in,
    w_mid_in,
    w_post_in,
    queries_in,
    w_key_in,
    w_value_in,
    features_out,
    landed,
    target_block,
    target_links,
    target_count,
    block_slot,
    points,
    positions,
    sn_positions,
    w_in,
    w_mid,
    w_post,
    queries,
    w_key,
    w_value,
    load_sem,
    pooled,
    features,
    values_t,
    keys,
    masked,
    peak_so_far,
    total_so_far,
    out_so_far,
    all_scores,
    all_probs,
    whole_features,
    parts,
    part_send,
    part_recv,
    arrived_a,
    arrived_b,
    sums_a,
    sums_b,
    block_of,
    wanted,
    everywhere,
    hidden,
    point_blocks,
    outgoing_a,
    outgoing_b,
    slots,
    pos_send,
    pos_recv,
    msg_send_a,
    msg_recv_a,
    msg_send_b,
    msg_recv_b,
    own_sem,
):
    me = place(n_sn)
    links = target_links.shape[0]
    width = points.shape[0]
    loads = [
        pltpu.make_async_copy(source, target, load_sem.at[i])
        for i, (source, target) in enumerate(
            [
                (target_block_in, target_block),
                (block_slot_in, block_slot),
                (target_count_in, target_count),
                (target_links_in, target_links),
                (sn_positions_in, sn_positions),
                (feats_in, points),
                (w_in_in, w_in),
                (w_mid_in, w_mid),
                (positions_in, positions),
                (w_post_in, w_post),
                (w_key_in, w_key),
                (w_value_in, w_value),
                (queries_in, queries),
            ]
        )
    ]
    for load in loads[:5]:
        load.start()
    barrier = greet(owners, me, n_sn)
    for load in loads[5:]:
        load.start()
    for load in loads[:5]:
        load.wait()

    def choose(region, carry):
        def slot_at(k):
            return block_slot[target_block[region * targets + k]]

        block = named_block(me, targets, sn_blocks, target_count[region], slot_at)[1]
        block_of[region] = block
        rows = sn_positions[:, :BLOCK]
        for b in range(1, sn_blocks):
            rows = jnp.where(block == b, sn_positions[:, b * BLOCK : (b + 1) * BLOCK], rows)
        wanted[region] = rows
        return carry

    lax.fori_loop(0, owners, choose, 0)

    def slot_of(k, carry):
        slots[k] = block_slot[target_block[me * targets + k]]
        return carry

    lax.fori_loop(0, targets, slot_of, 0)
    my_count = target_count[me]

    def pos_copy(other, slot_at):
        return pltpu.make_async_remote_copy(
            src_ref=wanted.at[other],
            dst_ref=everywhere.at[slot_at],
            send_sem=pos_send.at[other],
            recv_sem=pos_recv.at[slot_at],
            device_id=peer(other, n_sn),
            device_id_type=MESH,
        )

    def start_pos(i, carry):
        pos_copy(lax.rem(me + far_first(i, owners), owners), me).start()
        return carry

    def mlp(step, carry):
        span = pl.ds(pl.multiple_of(step * CHUNK, CHUNK), CHUNK)
        inner = jax.nn.gelu(contract(w_in[...], points[:, span], 0, 0)).astype(BF16)
        hid = contract(w_mid[...], inner, 0, 0).astype(BF16)
        places = positions[:, span]
        for q in range(CHUNK // BLOCK):
            hidden[step * (CHUNK // BLOCK) + q] = hid[:, q * BLOCK : (q + 1) * BLOCK]
            point_blocks[step * (CHUNK // BLOCK) + q] = places[:, q * BLOCK : (q + 1) * BLOCK]
        return carry

    mlp_steps = points.shape[1] // CHUNK
    for load in loads[5:9]:
        load.wait()
    early = early_steps(mlp_steps)
    lax.fori_loop(0, early, mlp, 0)
    pl.semaphore_wait(barrier, owners - 1)
    lax.fori_loop(0, owners - 1, start_pos, 0)
    own_pos = pltpu.make_async_copy(wanted.at[me], everywhere.at[me], own_sem.at[0])
    own_pos.start()
    lax.fori_loop(early, mlp_steps, mlp, 0)
    for load in loads[9:]:
        load.wait()

    outgoing = (outgoing_a, outgoing_b)
    arrived = (arrived_a, arrived_b)
    sums = (sums_a, sums_b)
    msg_send = (msg_send_a, msg_send_b)
    msg_recv = (msg_recv_a, msg_recv_b)
    half_rows = width // 2

    def msg_copy(p, other, slot_at):
        return pltpu.make_async_remote_copy(
            src_ref=outgoing[p].at[other],
            dst_ref=arrived[p].at[slot_at],
            send_sem=msg_send[p].at[other],
            recv_sem=msg_recv[p].at[slot_at],
            device_id=peer(other, n_sn),
            device_id_type=MESH,
        )

    def build(other):
        which, block, live = named_block(
            other, targets, sn_blocks, my_count, lambda k: slots[k]
        )
        sn_cols = columns_of(everywhere[other])
        kernels = []
        blocks = []
        for j in range(links):
            link = target_links[j, which]
            pts = point_blocks[link]
            dist = jnp.zeros((BLOCK, BLOCK), F32)
            for c in range(3):
                gap = sn_cols[:, c : c + 1] - pts[c : c + 1, :]
                dist = dist + gap * gap
            kernels.append(1.0 / (1.0 + dist * INV_RADIUS_SQ))
            blocks.append(hidden[link])
        total = kernels[0]
        for extra in kernels[1:]:
            total = total + extra
        total = jnp.sum(jnp.transpose(total), axis=0, keepdims=True)
        message = contract(
            jnp.concatenate(blocks, axis=1),
            jnp.concatenate([one.astype(BF16) for one in kernels], axis=1),
            1,
            1,
        )
        message = message * live
        halves = swap_halves(message[:half_rows], message[half_rows:])
        return (
            halves[0].astype(BF16),
            halves[1].astype(BF16),
            jnp.broadcast_to(total * live, (STAT_ROWS, BLOCK)).astype(BF16),
        )

    def nth(i):
        return lax.rem(me + far_first(i, owners), owners)

    def build_next(i, carry):
        other = nth(i)
        pos_copy(other, other).wait_recv()
        first_half, second_half, total = build(other)
        outgoing_a[other, :half_rows, :] = first_half
        outgoing_a[other, half_rows:, :] = total
        outgoing_b[other] = second_half
        msg_copy(0, other, me).start()
        return carry

    lax.fori_loop(0, owners - 1, build_next, 0)

    def send_second(i, carry):
        msg_copy(1, nth(i), me).start()
        return carry

    lax.fori_loop(0, owners - 1, send_second, 0)
    own_pos.wait()
    own_first, own_second, own_total = build(me)
    outgoing_a[me, :half_rows, :] = own_first
    outgoing_a[me, half_rows:, :] = own_total
    outgoing_b[me] = own_second

    def source_of(n):
        return lax.rem(me + n, owners)

    def gather(p):
        sums[p][...] = jnp.zeros(sums[p].shape, F32)

        def add(source, message):
            block = block_of[source]
            for b in range(sn_blocks):
                sums[p][b] += jnp.where(block == b, message, 0.0)

        add(me, outgoing[p][me].astype(F32))

        def arrive(n, carry):
            source = source_of(n)
            msg_copy(p, source, source).wait_recv()
            add(source, arrived[p][source].astype(F32))
            return carry

        lax.fori_loop(1, owners, arrive, 0)

    def pool(p):
        for pair in range(sn_blocks // 2):
            scaled = []
            for b in (2 * pair, 2 * pair + 1):
                total = sums_a[b][half_rows : half_rows + 1, :]
                scale = 1.0 / (1.0 + total)
                scale = swap_halves(scale, scale)[p]
                scaled.append(sums[p][b][:half_rows, :] * scale)
            upper, lower = swap_halves(scaled[0], scaled[1])
            columns = slice(pair * BLOCK, (pair + 1) * BLOCK)
            pooled[:half_rows, columns] = upper.astype(BF16)
            pooled[half_rows:, columns] = lower.astype(BF16)

    head_width = width // HEADS
    latents = queries.shape[1]
    share = latents // owners
    chunks = latents // LATENT_CHUNK
    per_chunk = LATENT_CHUNK // share
    row_head = lax.broadcasted_iota(jnp.int32, queries.shape, 0) // head_width
    scaled_queries = queries[...] * BF16(head_width ** (-0.5))
    for h in range(HEADS):
        masked[h] = jnp.where(row_head == h, scaled_queries, BF16(0.0))
    first = lax.div(me, per_chunk) + chunks // 2

    def project(p):
        pool(p)
        features[p] = jax.nn.gelu(contract(w_post[...], pooled[...], 0, 0)).astype(BF16)
        keys[...] = contract(features[p], w_key[...], 0, 0).astype(BF16)
        values_t[...] = contract(w_value[...], features[p], 0, 0).astype(BF16)

    def chunk_at(step):
        return lax.rem(first + step, chunks)

    def lanes_at(step, at, size):
        return pl.ds(pl.multiple_of(chunk_at(step) * LATENT_CHUNK + at, size), size)

    def score(step):
        inside = slice(step * LATENT_CHUNK, (step + 1) * LATENT_CHUNK)
        for h in range(HEADS):
            queries_h = masked[h, :, lanes_at(step, 0, LATENT_CHUNK)]
            all_scores[h, :, inside] = contract(keys[...], queries_h, 1, 0)

    def softmax(step, started):
        stats = []
        for h in range(HEADS):
            pieces = []
            for at in range(0, LATENT_CHUNK, BLOCK):
                inside = slice(step * LATENT_CHUNK + at, step * LATENT_CHUNK + at + BLOCK)
                lanes = lanes_at(step, at, BLOCK)
                scores = all_scores[h, :, inside]
                peak = jnp.max(scores, axis=0, keepdims=True)
                shrink = None
                if started:
                    old_peak = peak_so_far[h : h + 1, lanes]
                    peak = jnp.maximum(old_peak, peak)
                    shrink = jnp.exp(old_peak - peak)
                probs = jnp.exp(scores - peak)
                total = jnp.sum(probs, axis=0, keepdims=True)
                all_probs[h, :, inside] = probs.astype(BF16)
                if started:
                    total = total + shrink * total_so_far[h : h + 1, lanes]
                    pieces.append((peak, total, shrink))
                else:
                    peak_so_far[h : h + 1, lanes] = peak
                    total_so_far[h : h + 1, lanes] = total
            if started:
                stats.append([jnp.concatenate(kind, axis=1) for kind in zip(*pieces)])
        return stats

    def weigh(step, h):
        inside = slice(step * LATENT_CHUNK, (step + 1) * LATENT_CHUNK)
        own_values = values_t[h * head_width : (h + 1) * head_width, :]
        return contract(own_values, all_probs[h, :, inside], 1, 0)

    gather(0)
    project(0)
    for step in range(chunks):
        score(step)
    for step in range(chunks):
        softmax(step, False)
        for h in range(HEADS):
            rows = slice(h * head_width, (h + 1) * head_width)
            out_so_far[rows, lanes_at(step, 0, LATENT_CHUNK)] = weigh(step, h)
    gather(1)
    project(1)

    def attend(step):
        stats = softmax(step, True)
        outs, peaks, totals = [], [], []
        for h in range(HEADS):
            peak, total, shrink = stats[h]
            rows = slice(h * head_width, (h + 1) * head_width)
            outs.append(
                weigh(step, h) + shrink * out_so_far[rows, lanes_at(step, 0, LATENT_CHUNK)]
            )
            peaks += thirds(peak)
            totals += thirds(total)
        pad = jnp.zeros((OUT_LANES - width - 6 * HEADS, LATENT_CHUNK), F32)
        whole = jnp.concatenate(outs + peaks + totals + [pad], axis=0)
        whole = jnp.transpose(whole.astype(BF16))
        for j in range(per_chunk):
            parts[chunk_at(step) * per_chunk + j] = whole[j * share : (j + 1) * share, :]

    def copy_of(other, slot_at):
        return pltpu.make_async_remote_copy(
            src_ref=parts.at[other],
            dst_ref=landed.at[slot_at],
            send_sem=part_send.at[other],
            recv_sem=part_recv.at[slot_at],
            device_id=peer(other, n_sn),
            device_id_type=MESH,
        )

    def send_chunk(step):
        chunk = chunk_at(step)

        def start(j, carry):
            other = chunk * per_chunk + lax.rem(me + j, per_chunk)

            @pl.when(other != me)
            def _():
                copy_of(other, me).start()

            return carry

        lax.fori_loop(0, per_chunk, start, 0)

    for step in range(chunks):
        score(step)
    for step in range(chunks):
        attend(step)
        send_chunk(step)
    own = pltpu.make_async_copy(parts.at[me], landed.at[me], own_sem.at[1])
    own.start()
    for pair in range(sn_blocks // 2):
        columns = slice(pair * BLOCK, (pair + 1) * BLOCK)
        whole = swap_halves(features[0, :, columns].astype(F32), features[1, :, columns].astype(F32))
        for side in range(2):
            at = (2 * pair + side) * BLOCK
            whole_features[:, at : at + BLOCK] = whole[side].astype(BF16)
    store = pltpu.make_async_copy(whole_features, features_out, own_sem.at[2])
    store.start()

    def sent(i, carry):
        msg_copy(0, nth(i), nth(i)).wait_send()
        msg_copy(1, nth(i), nth(i)).wait_send()
        pos_copy(nth(i), nth(i)).wait_send()
        return carry

    lax.fori_loop(0, owners - 1, sent, 0)
    own.wait()

    def settle(off, carry):
        other = lax.rem(me + off, owners)
        copy = copy_of(other, other)
        copy.wait_send()
        copy.wait_recv()
        return carry

    lax.fori_loop(1, owners, settle, 0)
    store.wait()


def finish_kernel(features_in, landed, w_out, out_gain, features, latent_out, sem):
    move = pltpu.make_async_copy(features_in, features, sem)
    move.start()
    owners, share, _ = landed.shape
    width = w_out.shape[0]
    head_width = width // HEADS
    lane = lax.broadcasted_iota(jnp.int32, (OUT_LANES, width), 0) - width
    head_of = lax.broadcasted_iota(jnp.int32, (OUT_LANES, width), 1) // head_width
    is_peak = jnp.logical_and(lane >= 3 * head_of, lane < 3 * head_of + 3)
    total_lane = lane - 3 * HEADS
    is_total = jnp.logical_and(total_lane >= 3 * head_of, total_lane < 3 * head_of + 3)
    flat = jnp.concatenate([landed[source] for source in range(owners)], axis=0)
    peaks = contract(flat, jnp.where(is_peak, 1.0, 0.0).astype(BF16), 1, 0)
    totals = contract(flat, jnp.where(is_total, 1.0, 0.0).astype(BF16), 1, 0)

    def of(full, source):
        return full[source * share : (source + 1) * share, :]

    top = of(peaks, 0)
    for source in range(1, owners):
        top = jnp.maximum(top, of(peaks, source))
    output = jnp.zeros((share, width), F32)
    total = jnp.zeros((share, width), F32)
    for source in range(owners):
        scale = jnp.exp(of(peaks, source) - top)
        output = output + scale * landed[source][:, :width].astype(F32)
        total = total + scale * of(totals, source)
    attended = (output / total).astype(BF16)
    projected = jnp.dot(attended, w_out[...], preferred_element_type=F32)
    mean_sq = jnp.mean(projected * projected, axis=-1, keepdims=True)
    normed = projected * lax.rsqrt(mean_sq + 1e-06)
    latent_out[...] = (normed * out_gain[...]).astype(BF16)
    move.wait()


def per_device(
    n_sn,
    owners,
    point_features,
    point_positions,
    sn_positions,
    latent_queries,
    target_block,
    target_links,
    target_count,
    block_slot,
    w_in,
    w_mid,
    w_post,
    w_key,
    w_value,
    w_out,
    out_gain,
):
    targets = target_links.shape[0]
    width = point_features.shape[1]
    sn_rows = sn_positions.shape[1]
    sn_blocks = sn_rows // BLOCK
    latents = latent_queries.shape[0]
    share = latents // owners
    vmem = pl.BlockSpec(memory_space=pltpu.VMEM)
    hbm = pl.BlockSpec(memory_space=pl.ANY)
    dma = pltpu.SemaphoreType.DMA
    points = point_features.shape[0]
    rows_a = width // 2 + STAT_ROWS
    features_t, landed = pl.pallas_call(
        functools.partial(encoder_kernel, owners, n_sn, sn_blocks, targets),
        out_shape=(
            jax.ShapeDtypeStruct((width, sn_rows), BF16),
            jax.ShapeDtypeStruct((owners, share, OUT_LANES), BF16),
        ),
        in_specs=[hbm] * 13,
        out_specs=(hbm, hbm),
        scratch_shapes=[
            pltpu.SMEM(target_block.shape, jnp.int32),
            pltpu.SMEM(target_links.shape[::-1], jnp.int32),
            pltpu.SMEM(target_count.shape, jnp.int32),
            pltpu.SMEM(block_slot.shape, jnp.int32),
            pltpu.VMEM((width, points), BF16),
            pltpu.VMEM(point_positions.shape, F32),
            pltpu.VMEM(sn_positions.shape, F32),
            pltpu.VMEM(w_in.shape, BF16),
            pltpu.VMEM(w_mid.shape, BF16),
            pltpu.VMEM(w_post.shape, BF16),
            pltpu.VMEM(latent_queries.shape[::-1], BF16),
            pltpu.VMEM(w_key.shape, BF16),
            pltpu.VMEM(w_value.shape, BF16),
            dma((13,)),
            pltpu.VMEM((width, sn_rows // 2), BF16),
            pltpu.VMEM((2, width, sn_rows // 2), BF16),
            pltpu.VMEM((width, sn_rows // 2), BF16),
            pltpu.VMEM((sn_rows // 2, width), BF16),
            pltpu.VMEM((HEADS, width, latents), BF16),
            pltpu.VMEM((HEADS, latents), F32),
            pltpu.VMEM((HEADS, latents), F32),
            pltpu.VMEM((width, latents), F32),
            pltpu.VMEM((HEADS, sn_rows // 2, latents), F32),
            pltpu.VMEM((HEADS, sn_rows // 2, latents), BF16),
            pltpu.VMEM((width, sn_rows), BF16),
            pltpu.VMEM((owners, share, OUT_LANES), BF16),
            dma((owners,)),
            dma((owners,)),
            pltpu.VMEM((owners, rows_a, BLOCK), BF16),
            pltpu.VMEM((owners, width // 2, BLOCK), BF16),
            pltpu.VMEM((sn_blocks, rows_a, BLOCK), F32),
            pltpu.VMEM((sn_blocks, width // 2, BLOCK), F32),
            pltpu.SMEM((owners,), jnp.int32),
            pltpu.VMEM((owners, 3, BLOCK), F32),
            pltpu.VMEM((owners, 3, BLOCK), F32),
            pltpu.VMEM((points // BLOCK, width, BLOCK), BF16),
            pltpu.VMEM((points // BLOCK, 3, BLOCK), F32),
            pltpu.VMEM((owners, rows_a, BLOCK), BF16),
            pltpu.VMEM((owners, width // 2, BLOCK), BF16),
            pltpu.SMEM((targets,), jnp.int32),
            dma((owners,)),
            dma((owners,)),
            dma((owners,)),
            dma((owners,)),
            dma((owners,)),
            dma((owners,)),
            dma((3,)),
        ],
        compiler_params=pltpu.CompilerParams(
            collective_id=0, has_side_effects=True, vmem_limit_bytes=VMEM_LIMIT
        ),
        name="encoder",
    )(
        *(
            pltpu.with_memory_space_constraint(operand, pltpu.HBM)
            for operand in (
                target_block,
                target_links.T,
                target_count,
                block_slot,
                point_features.T,
                point_positions,
                sn_positions,
                w_in,
                w_mid,
                w_post,
                latent_queries.T,
                w_key,
                w_value,
            )
        )
    )
    features_t, latent_out = pl.pallas_call(
        finish_kernel,
        out_shape=(
            jax.ShapeDtypeStruct((width, sn_rows), BF16),
            jax.ShapeDtypeStruct((share, width), BF16),
        ),
        in_specs=[hbm] + [vmem] * 3,
        out_specs=(hbm, vmem),
        scratch_shapes=[dma],
        compiler_params=pltpu.CompilerParams(vmem_limit_bytes=VMEM_LIMIT),
        name="finish",
    )(features_t, landed, w_out, out_gain.reshape(1, width))
    return (features_t.T, latent_out)


def solution(mesh):
    n_sn = mesh.shape["sn"]
    owners = mesh.shape["pts"] * n_sn
    everything = ("groups", "pts", "sn")
    in_specs = (
        P(everything, None),
        P(None, everything),
        P(None, everything),
        P(),
        P("groups"),
        P(everything, None),
        P("groups"),
        P("groups"),
        P(),
        P(),
        P(),
        P(),
        P(),
        P(),
        P(),
    )
    out_specs = (P(everything, None), P(everything, None))
    return jax.shard_map(
        functools.partial(per_device, n_sn, owners),
        mesh=mesh,
        in_specs=in_specs,
        out_specs=out_specs,
        check_vma=False,
    )
```

```python
import functools

import jax
import jax.numpy as jnp
from jax import lax
from jax.experimental import pallas as pl
from jax.experimental.pallas import tpu as pltpu
from jax.sharding import PartitionSpec as P

HEADS = 3
BLOCK = 128
INV_RADIUS_SQ = 100.0
MESH = pl.DeviceIdType.MESH
STAT_ROWS = 8
CHUNK = 2048
OUT_LANES = 256
VMEM_LIMIT = 40 * 2**20
F32 = jnp.float32
BF16 = jnp.bfloat16


def contract(a, b, dim_a, dim_b):
    return lax.dot_general(a, b, (((dim_a,), (dim_b,)), ((), ())), preferred_element_type=F32)


def place(n_sn):
    return lax.axis_index("pts") * n_sn + lax.axis_index("sn")


def peer(index, n_sn):
    return {"pts": lax.div(index, n_sn), "sn": lax.rem(index, n_sn)}


def greet(owners, me, n_sn):
    barrier = pltpu.get_barrier_semaphore()

    def signal(off, carry):
        other = lax.rem(me + off, owners)
        pl.semaphore_signal(barrier, inc=1, device_id=peer(other, n_sn), device_id_type=MESH)
        return carry

    lax.fori_loop(1, owners, signal, 0)
    return barrier


def early_steps(steps):
    left = 3 - lax.div(lax.axis_index("pts") * 4, lax.axis_size("pts"))
    return steps // 2 * lax.div(left * left, 4)


def across_first(me, i, owners):
    left = owners - 1 - i
    top = 1
    bit = 2
    while bit < owners:
        top = jnp.where(left >= bit, bit, top)
        bit *= 2
    offset = 3 * top - 1 - left
    other = 0
    bit = 1
    while bit < owners:
        other = other + bit * lax.rem(lax.div(me, bit) + lax.div(offset, bit), 2)
        bit *= 2
    return other


def named_block(owner, targets, sn_blocks, count, slot_at):
    def look(k, state):
        which, block, live = state
        slot = slot_at(k)
        hit = jnp.logical_and(lax.div(slot, sn_blocks) == owner, k < count)
        return (
            jnp.where(hit, k, which),
            jnp.where(hit, lax.rem(slot, sn_blocks), block),
            jnp.where(hit, 1.0, live),
        )

    start = (jnp.int32(0), jnp.int32(0), F32(0.0))
    return lax.fori_loop(0, targets, look, start, unroll=targets <= 8)


def low_lanes(shape):
    return lax.broadcasted_iota(jnp.int32, shape, 1) < BLOCK // 2


def swap_halves(upper, lower):
    low = low_lanes(upper.shape)
    half = BLOCK // 2
    return (
        jnp.where(low, upper, pltpu.roll(lower, half, 1)),
        jnp.where(low, pltpu.roll(upper, half, 1), lower),
    )


def columns_of(rows):
    padded = jnp.concatenate([rows, jnp.zeros((5, rows.shape[1]), F32)], axis=0)
    return jnp.transpose(padded)


def thirds(x):
    first = x.astype(BF16).astype(F32)
    second = (x - first).astype(BF16).astype(F32)
    third = x - first - second
    return [first, second, third]


def encoder_kernel(
    owners,
    n_sn,
    sn_blocks,
    targets,
    target_block_in,
    target_links_in,
    target_count_in,
    block_slot_in,
    feats_in,
    positions_in,
    sn_positions_in,
    w_in_in,
    w_mid_in,
    w_post_in,
    queries_in,
    w_key_in,
    w_value_in,
    features_out,
    landed,
    target_block,
    target_links,
    target_count,
    block_slot,
    points,
    positions,
    sn_positions,
    w_in,
    w_mid,
    w_post,
    queries,
    w_key,
    w_value,
    load_sem,
    pooled,
    features,
    values_t,
    keys,
    masked,
    peak_so_far,
    total_so_far,
    out_so_far,
    all_scores,
    all_probs,
    whole_features,
    parts,
    part_send,
    part_recv,
    pair_out,
    pair_in,
    pair_sem,
    arrived_a,
    arrived_b,
    sums_a,
    sums_b,
    block_of,
    wanted,
    everywhere,
    hidden,
    point_blocks,
    outgoing_a,
    outgoing_b,
    slots,
    pos_send,
    pos_recv,
    msg_send_a,
    msg_recv_a,
    msg_send_b,
    msg_recv_b,
    own_sem,
):
    me = place(n_sn)
    links = target_links.shape[0]
    width = points.shape[0]
    loads = [
        pltpu.make_async_copy(source, target, load_sem.at[i])
        for i, (source, target) in enumerate(
            [
                (target_block_in, target_block),
                (block_slot_in, block_slot),
                (target_count_in, target_count),
                (target_links_in, target_links),
                (sn_positions_in, sn_positions),
                (feats_in, points),
                (w_in_in, w_in),
                (w_mid_in, w_mid),
                (positions_in, positions),
                (w_post_in, w_post),
                (w_key_in, w_key),
                (w_value_in, w_value),
                (queries_in, queries),
            ]
        )
    ]
    for load in loads[:5]:
        load.start()
    barrier = greet(owners, me, n_sn)
    for load in loads[5:]:
        load.start()
    for load in loads[:5]:
        load.wait()

    def choose(region, carry):
        def slot_at(k):
            return block_slot[target_block[region * targets + k]]

        block = named_block(me, targets, sn_blocks, target_count[region], slot_at)[1]
        block_of[region] = block
        rows = sn_positions[:, :BLOCK]
        for b in range(1, sn_blocks):
            rows = jnp.where(block == b, sn_positions[:, b * BLOCK : (b + 1) * BLOCK], rows)
        wanted[region] = rows
        return carry

    lax.fori_loop(0, owners, choose, 0, unroll=4)

    def slot_of(k, carry):
        slots[k] = block_slot[target_block[me * targets + k]]
        return carry

    lax.fori_loop(0, targets, slot_of, 0)
    my_count = target_count[me]

    def pos_copy(other, slot_at):
        return pltpu.make_async_remote_copy(
            src_ref=wanted.at[other],
            dst_ref=everywhere.at[slot_at],
            send_sem=pos_send.at[other],
            recv_sem=pos_recv.at[slot_at],
            device_id=peer(other, n_sn),
            device_id_type=MESH,
        )

    def start_pos(i, carry):
        pos_copy(across_first(me, i, owners), me).start()
        return carry

    def mlp(step, carry):
        span = pl.ds(pl.multiple_of(step * CHUNK, CHUNK), CHUNK)
        inner = jax.nn.gelu(contract(w_in[...], points[:, span], 0, 0)).astype(BF16)
        hid = contract(w_mid[...], inner, 0, 0).astype(BF16)
        places = positions[:, span]
        for q in range(CHUNK // BLOCK):
            hidden[step * (CHUNK // BLOCK) + q] = hid[:, q * BLOCK : (q + 1) * BLOCK]
            point_blocks[step * (CHUNK // BLOCK) + q] = places[:, q * BLOCK : (q + 1) * BLOCK]
        return carry

    mlp_steps = points.shape[1] // CHUNK
    for load in loads[5:9]:
        load.wait()
    early = early_steps(mlp_steps)
    lax.fori_loop(0, early, mlp, 0)
    pl.semaphore_wait(barrier, owners - 1)
    lax.fori_loop(0, owners - 1, start_pos, 0)
    own_pos = pltpu.make_async_copy(wanted.at[me], everywhere.at[me], own_sem.at[0])
    own_pos.start()
    lax.fori_loop(early, mlp_steps, mlp, 0)
    for load in loads[9:]:
        load.wait()

    outgoing = (outgoing_a, outgoing_b)
    arrived = (arrived_a, arrived_b)
    sums = (sums_a, sums_b)
    msg_send = (msg_send_a, msg_send_b)
    msg_recv = (msg_recv_a, msg_recv_b)
    half_rows = width // 2

    def msg_copy(p, other, slot_at):
        return pltpu.make_async_remote_copy(
            src_ref=outgoing[p].at[other],
            dst_ref=arrived[p].at[slot_at],
            send_sem=msg_send[p].at[other],
            recv_sem=msg_recv[p].at[slot_at],
            device_id=peer(other, n_sn),
            device_id_type=MESH,
        )

    def build(other):
        which, block, live = named_block(
            other, targets, sn_blocks, my_count, lambda k: slots[k]
        )
        sn_cols = columns_of(everywhere[other])
        kernels = []
        blocks = []
        for j in range(links):
            link = target_links[j, which]
            pts = point_blocks[link]
            dist = jnp.zeros((BLOCK, BLOCK), F32)
            for c in range(3):
                gap = sn_cols[:, c : c + 1] - pts[c : c + 1, :]
                dist = dist + gap * gap
            kernels.append(1.0 / (1.0 + dist * INV_RADIUS_SQ))
            blocks.append(hidden[link])
        total = kernels[0]
        for extra in kernels[1:]:
            total = total + extra
        total = jnp.sum(jnp.transpose(total), axis=0, keepdims=True)
        message = contract(
            jnp.concatenate(blocks, axis=1),
            jnp.concatenate([one.astype(BF16) for one in kernels], axis=1),
            1,
            1,
        )
        message = message * live
        halves = swap_halves(message[:half_rows], message[half_rows:])
        return (
            halves[0].astype(BF16),
            halves[1].astype(BF16),
            jnp.broadcast_to(total * live, (STAT_ROWS, BLOCK)).astype(BF16),
        )

    def nth(i):
        return across_first(me, i, owners)

    def build_next(i, carry):
        other = nth(i)
        pos_copy(other, other).wait_recv()
        first_half, second_half, total = build(other)
        outgoing_a[other, :half_rows, :] = first_half
        outgoing_a[other, half_rows:, :] = total
        outgoing_b[other] = second_half
        msg_copy(0, other, me).start()
        return carry

    lax.fori_loop(0, owners - 1, build_next, 0)

    def send_second(i, carry):
        msg_copy(1, nth(i), me).start()
        return carry

    lax.fori_loop(0, owners - 1, send_second, 0)
    own_pos.wait()
    own_first, own_second, own_total = build(me)
    outgoing_a[me, :half_rows, :] = own_first
    outgoing_a[me, half_rows:, :] = own_total
    outgoing_b[me] = own_second

    def source_of(n):
        return lax.rem(me + n, owners)

    def gather(p):
        sums[p][...] = jnp.zeros(sums[p].shape, F32)

        def add(source, message):
            block = block_of[source]
            for b in range(sn_blocks):
                sums[p][b] += jnp.where(block == b, message, 0.0)

        add(me, outgoing[p][me].astype(F32))

        def arrive(n, carry):
            source = source_of(n)
            msg_copy(p, source, source).wait_recv()
            add(source, arrived[p][source].astype(F32))
            return carry

        lax.fori_loop(1, owners, arrive, 0)

    def pool(p):
        for pair in range(sn_blocks // 2):
            scaled = []
            for b in (2 * pair, 2 * pair + 1):
                total = sums_a[b][half_rows : half_rows + 1, :]
                scale = 1.0 / (1.0 + total)
                scale = swap_halves(scale, scale)[p]
                scaled.append(sums[p][b][:half_rows, :] * scale)
            upper, lower = swap_halves(scaled[0], scaled[1])
            columns = slice(pair * BLOCK, (pair + 1) * BLOCK)
            pooled[:half_rows, columns] = upper.astype(BF16)
            pooled[half_rows:, columns] = lower.astype(BF16)

    head_width = width // HEADS
    latents = queries.shape[1]
    share = latents // owners
    group = latents // n_sn
    places = owners // n_sn
    my_pts = lax.axis_index("pts")
    my_sn = lax.axis_index("sn")
    row_head = lax.broadcasted_iota(jnp.int32, queries.shape, 0) // head_width
    column = lax.broadcasted_iota(jnp.int32, (latents, latents), 1)
    inside_group = column % group
    taken = (inside_group // share * n_sn + column // group) * share + inside_group % share
    pick = lax.broadcasted_iota(jnp.int32, (latents, latents), 0) == taken
    by_core = contract(queries[...], jnp.where(pick, 1.0, 0.0).astype(BF16), 1, 0).astype(BF16)
    scaled_queries = by_core * BF16(head_width ** (-0.5))
    for h in range(HEADS):
        masked[h] = jnp.where(row_head == h, scaled_queries, BF16(0.0))

    def project(p):
        pool(p)
        features[p] = jax.nn.gelu(contract(w_post[...], pooled[...], 0, 0)).astype(BF16)
        keys[...] = contract(features[p], w_key[...], 0, 0).astype(BF16)
        values_t[...] = contract(w_value[...], features[p], 0, 0).astype(BF16)

    def chunk_at(step):
        return lax.rem(my_sn + 1 + step, n_sn)

    def lanes_at(step, at, size):
        return pl.ds(pl.multiple_of(chunk_at(step) * group + at, size), size)

    def score(step):
        inside = slice(step * group, (step + 1) * group)
        for h in range(HEADS):
            queries_h = masked[h, :, lanes_at(step, 0, group)]
            all_scores[h, :, inside] = contract(keys[...], queries_h, 1, 0)

    def softmax(step, started):
        stats = []
        for h in range(HEADS):
            pieces = []
            for at in range(0, group, BLOCK):
                inside = slice(step * group + at, step * group + at + BLOCK)
                lanes = lanes_at(step, at, BLOCK)
                scores = all_scores[h, :, inside]
                peak = jnp.max(scores, axis=0, keepdims=True)
                shrink = None
                if started:
                    old_peak = peak_so_far[h : h + 1, lanes]
                    peak = jnp.maximum(old_peak, peak)
                    shrink = jnp.exp(old_peak - peak)
                probs = jnp.exp(scores - peak)
                total = jnp.sum(probs, axis=0, keepdims=True)
                all_probs[h, :, inside] = probs.astype(BF16)
                if started:
                    total = total + shrink * total_so_far[h : h + 1, lanes]
                    pieces.append((peak, total, shrink))
                else:
                    peak_so_far[h : h + 1, lanes] = peak
                    total_so_far[h : h + 1, lanes] = total
            if started:
                stats.append([jnp.concatenate(kind, axis=1) for kind in zip(*pieces)])
        return stats

    def weigh(step, h):
        inside = slice(step * group, (step + 1) * group)
        own_values = values_t[h * head_width : (h + 1) * head_width, :]
        return contract(own_values, all_probs[h, :, inside], 1, 0)

    gather(0)
    project(0)
    for step in range(n_sn):
        score(step)
    for step in range(n_sn):
        softmax(step, False)
        for h in range(HEADS):
            rows = slice(h * head_width, (h + 1) * head_width)
            out_so_far[rows, lanes_at(step, 0, group)] = weigh(step, h)
    gather(1)
    project(1)

    def attend(step):
        stats = softmax(step, True)
        state = []
        for h in range(HEADS):
            peak, total, shrink = stats[h]
            rows = slice(h * head_width, (h + 1) * head_width)
            out = weigh(step, h) + shrink * out_so_far[rows, lanes_at(step, 0, group)]
            state.append((peak, total, out))
        return state

    def pair_copy():
        return pltpu.make_async_remote_copy(
            src_ref=pair_out,
            dst_ref=pair_in,
            send_sem=pair_sem.at[0],
            recv_sem=pair_sem.at[1],
            device_id={"pts": my_pts, "sn": 1 - my_sn},
            device_id_type=MESH,
        )

    def copy_of(other, slot_at):
        return pltpu.make_async_remote_copy(
            src_ref=parts.at[other],
            dst_ref=landed.at[slot_at],
            send_sem=part_send.at[other],
            recv_sem=part_recv.at[slot_at],
            device_id={"pts": other, "sn": my_sn},
            device_id_type=MESH,
        )

    for step in range(n_sn):
        score(step)
    for h, (peak, total, out) in enumerate(attend(0)):
        pair_out[h * head_width : (h + 1) * head_width, :] = out
        pair_out[width + h : width + h + 1, :] = peak
        pair_out[width + HEADS + h : width + HEADS + h + 1, :] = total
    pair_out[width + 2 * HEADS :, :] = jnp.zeros((8 - 2 * HEADS, group), F32)
    pair_copy().start()
    mine = attend(1)
    pair_copy().wait_recv()
    outs, peaks, totals = [], [], []
    for h, (peak, total, out) in enumerate(mine):
        their_peak = pair_in[width + h : width + h + 1, :]
        their_total = pair_in[width + HEADS + h : width + HEADS + h + 1, :]
        top = jnp.maximum(peak, their_peak)
        shrink = jnp.exp(peak - top)
        their_shrink = jnp.exp(their_peak - top)
        peaks += thirds(top)
        totals += thirds(total * shrink + their_total * their_shrink)
        theirs = pair_in[h * head_width : (h + 1) * head_width, :]
        outs.append(out * shrink + theirs * their_shrink)
    pad = jnp.zeros((OUT_LANES - width - 6 * HEADS, group), F32)
    merged = jnp.concatenate(outs + peaks + totals + [pad], axis=0)
    merged = jnp.transpose(merged.astype(BF16))
    for j in range(places):
        parts[j] = merged[j * share : (j + 1) * share, :]

    def send_part(i, carry):
        copy_of(across_first(my_pts, i, places), my_pts).start()
        return carry

    lax.fori_loop(0, places - 1, send_part, 0)
    own = pltpu.make_async_copy(parts.at[my_pts], landed.at[my_pts], own_sem.at[1])
    own.start()
    for pair in range(sn_blocks // 2):
        columns = slice(pair * BLOCK, (pair + 1) * BLOCK)
        whole = swap_halves(features[0, :, columns].astype(F32), features[1, :, columns].astype(F32))
        for side in range(2):
            at = (2 * pair + side) * BLOCK
            whole_features[:, at : at + BLOCK] = whole[side].astype(BF16)
    store = pltpu.make_async_copy(whole_features, features_out, own_sem.at[2])
    store.start()

    def sent(i, carry):
        msg_copy(0, nth(i), nth(i)).wait_send()
        msg_copy(1, nth(i), nth(i)).wait_send()
        pos_copy(nth(i), nth(i)).wait_send()
        return carry

    lax.fori_loop(0, owners - 1, sent, 0)
    pair_copy().wait_send()
    own.wait()

    def settle(off, carry):
        other = lax.rem(my_pts + off, places)
        copy = copy_of(other, other)
        copy.wait_send()
        copy.wait_recv()
        return carry

    lax.fori_loop(1, places, settle, 0)
    store.wait()


def finish_kernel(features_in, landed, w_out, out_gain, features, latent_out, sem):
    move = pltpu.make_async_copy(features_in, features, sem)
    move.start()
    owners, share, _ = landed.shape
    width = w_out.shape[0]
    head_width = width // HEADS
    lane = lax.broadcasted_iota(jnp.int32, (OUT_LANES, width), 0) - width
    head_of = lax.broadcasted_iota(jnp.int32, (OUT_LANES, width), 1) // head_width
    is_peak = jnp.logical_and(lane >= 3 * head_of, lane < 3 * head_of + 3)
    total_lane = lane - 3 * HEADS
    is_total = jnp.logical_and(total_lane >= 3 * head_of, total_lane < 3 * head_of + 3)
    flat = jnp.concatenate([landed[source] for source in range(owners)], axis=0)
    peaks = contract(flat, jnp.where(is_peak, 1.0, 0.0).astype(BF16), 1, 0)
    totals = contract(flat, jnp.where(is_total, 1.0, 0.0).astype(BF16), 1, 0)

    def of(full, source):
        return full[source * share : (source + 1) * share, :]

    top = of(peaks, 0)
    for source in range(1, owners):
        top = jnp.maximum(top, of(peaks, source))
    output = jnp.zeros((share, width), F32)
    total = jnp.zeros((share, width), F32)
    for source in range(owners):
        scale = jnp.exp(of(peaks, source) - top)
        output = output + scale * landed[source][:, :width].astype(F32)
        total = total + scale * of(totals, source)
    attended = (output / total).astype(BF16)
    projected = jnp.dot(attended, w_out[...], preferred_element_type=F32)
    mean_sq = jnp.mean(projected * projected, axis=-1, keepdims=True)
    normed = projected * lax.rsqrt(mean_sq + 1e-06)
    latent_out[...] = (normed * out_gain[...]).astype(BF16)
    move.wait()


def per_device(
    n_sn,
    owners,
    point_features,
    point_positions,
    sn_positions,
    latent_queries,
    target_block,
    target_links,
    target_count,
    block_slot,
    w_in,
    w_mid,
    w_post,
    w_key,
    w_value,
    w_out,
    out_gain,
):
    targets = target_links.shape[0]
    width = point_features.shape[1]
    sn_rows = sn_positions.shape[1]
    sn_blocks = sn_rows // BLOCK
    latents = latent_queries.shape[0]
    share = latents // owners
    vmem = pl.BlockSpec(memory_space=pltpu.VMEM)
    hbm = pl.BlockSpec(memory_space=pl.ANY)
    dma = pltpu.SemaphoreType.DMA
    points = point_features.shape[0]
    rows_a = width // 2 + STAT_ROWS
    features_t, landed = pl.pallas_call(
        functools.partial(encoder_kernel, owners, n_sn, sn_blocks, targets),
        out_shape=(
            jax.ShapeDtypeStruct((width, sn_rows), BF16),
            jax.ShapeDtypeStruct((owners // n_sn, share, OUT_LANES), BF16),
        ),
        in_specs=[hbm] * 13,
        out_specs=(hbm, hbm),
        scratch_shapes=[
            pltpu.SMEM(target_block.shape, jnp.int32),
            pltpu.SMEM(target_links.shape[::-1], jnp.int32),
            pltpu.SMEM(target_count.shape, jnp.int32),
            pltpu.SMEM(block_slot.shape, jnp.int32),
            pltpu.VMEM((width, points), BF16),
            pltpu.VMEM(point_positions.shape, F32),
            pltpu.VMEM(sn_positions.shape, F32),
            pltpu.VMEM(w_in.shape, BF16),
            pltpu.VMEM(w_mid.shape, BF16),
            pltpu.VMEM(w_post.shape, BF16),
            pltpu.VMEM(latent_queries.shape[::-1], BF16),
            pltpu.VMEM(w_key.shape, BF16),
            pltpu.VMEM(w_value.shape, BF16),
            dma((13,)),
            pltpu.VMEM((width, sn_rows // 2), BF16),
            pltpu.VMEM((2, width, sn_rows // 2), BF16),
            pltpu.VMEM((width, sn_rows // 2), BF16),
            pltpu.VMEM((sn_rows // 2, width), BF16),
            pltpu.VMEM((HEADS, width, latents), BF16),
            pltpu.VMEM((HEADS, latents), F32),
            pltpu.VMEM((HEADS, latents), F32),
            pltpu.VMEM((width, latents), F32),
            pltpu.VMEM((HEADS, sn_rows // 2, latents), F32),
            pltpu.VMEM((HEADS, sn_rows // 2, latents), BF16),
            pltpu.VMEM((width, sn_rows), BF16),
            pltpu.VMEM((owners // n_sn, share, OUT_LANES), BF16),
            dma((owners // n_sn,)),
            dma((owners // n_sn,)),
            pltpu.VMEM((width + 8, latents // n_sn), F32),
            pltpu.VMEM((width + 8, latents // n_sn), F32),
            dma((2,)),
            pltpu.VMEM((owners, rows_a, BLOCK), BF16),
            pltpu.VMEM((owners, width // 2, BLOCK), BF16),
            pltpu.VMEM((sn_blocks, rows_a, BLOCK), F32),
            pltpu.VMEM((sn_blocks, width // 2, BLOCK), F32),
            pltpu.SMEM((owners,), jnp.int32),
            pltpu.VMEM((owners, 3, BLOCK), F32),
            pltpu.VMEM((owners, 3, BLOCK), F32),
            pltpu.VMEM((points // BLOCK, width, BLOCK), BF16),
            pltpu.VMEM((points // BLOCK, 3, BLOCK), F32),
            pltpu.VMEM((owners, rows_a, BLOCK), BF16),
            pltpu.VMEM((owners, width // 2, BLOCK), BF16),
            pltpu.SMEM((targets,), jnp.int32),
            dma((owners,)),
            dma((owners,)),
            dma((owners,)),
            dma((owners,)),
            dma((owners,)),
            dma((owners,)),
            dma((3,)),
        ],
        compiler_params=pltpu.CompilerParams(
            collective_id=0, has_side_effects=True, vmem_limit_bytes=VMEM_LIMIT
        ),
        name="encoder",
    )(
        *(
            pltpu.with_memory_space_constraint(operand, pltpu.HBM)
            for operand in (
                target_block,
                target_links.T,
                target_count,
                block_slot,
                point_features.T,
                point_positions,
                sn_positions,
                w_in,
                w_mid,
                w_post,
                latent_queries.T,
                w_key,
                w_value,
            )
        )
    )
    features_t, latent_out = pl.pallas_call(
        finish_kernel,
        out_shape=(
            jax.ShapeDtypeStruct((width, sn_rows), BF16),
            jax.ShapeDtypeStruct((share, width), BF16),
        ),
        in_specs=[hbm] + [vmem] * 3,
        out_specs=(hbm, vmem),
        scratch_shapes=[dma],
        compiler_params=pltpu.CompilerParams(vmem_limit_bytes=VMEM_LIMIT),
        name="finish",
    )(features_t, landed, w_out, out_gain.reshape(1, width))
    return (features_t.T, latent_out)


def solution(mesh):
    n_sn = mesh.shape["sn"]
    owners = mesh.shape["pts"] * n_sn
    everything = ("groups", "pts", "sn")
    in_specs = (
        P(everything, None),
        P(None, everything),
        P(None, everything),
        P(),
        P("groups"),
        P(everything, None),
        P("groups"),
        P("groups"),
        P(),
        P(),
        P(),
        P(),
        P(),
        P(),
        P(),
    )
    out_specs = (P(everything, None), P(everything, None))
    return jax.shard_map(
        functools.partial(per_device, n_sn, owners),
        mesh=mesh,
        in_specs=in_specs,
        out_specs=out_specs,
        check_vma=False,
    )
```

```python
import functools

import jax
import jax.numpy as jnp
from jax import lax
from jax.experimental import pallas as pl
from jax.experimental.pallas import tpu as pltpu
from jax.sharding import PartitionSpec as P

HEADS = 3
BLOCK = 128
INV_RADIUS_SQ = 100.0
MESH = pl.DeviceIdType.MESH
STAT_ROWS = 8
CHUNK = 2048
OUT_LANES = 256
VMEM_LIMIT = 40 * 2**20
F32 = jnp.float32
BF16 = jnp.bfloat16


def contract(a, b, dim_a, dim_b):
    return lax.dot_general(a, b, (((dim_a,), (dim_b,)), ((), ())), preferred_element_type=F32)


def place(n_sn):
    return lax.axis_index("pts") * n_sn + lax.axis_index("sn")


def peer(index, n_sn):
    return {"pts": lax.div(index, n_sn), "sn": lax.rem(index, n_sn)}


def greet(owners, me, n_sn):
    barrier = pltpu.get_barrier_semaphore()

    def signal(i, carry):
        other = across_first(me, i, owners)
        pl.semaphore_signal(barrier, inc=1, device_id=peer(other, n_sn), device_id_type=MESH)
        return carry

    lax.fori_loop(0, owners - 1, signal, 0, unroll=owners <= 16)
    return barrier


def early_steps(steps):
    left = 3 - lax.div(lax.axis_index("pts") * 4, lax.axis_size("pts"))
    return steps // 2 * lax.div(left * left, 4)


def across_first(me, i, owners):
    left = owners - 1 - i
    top = 1
    bit = 2
    while bit < owners:
        top = jnp.where(left >= bit, bit, top)
        bit *= 2
    offset = 3 * top - 1 - left
    other = 0
    bit = 1
    while bit < owners:
        other = other + bit * lax.rem(lax.div(me, bit) + lax.div(offset, bit), 2)
        bit *= 2
    return other


def named_block(owner, targets, sn_blocks, count, slot_at):
    def look(k, state):
        which, block, live = state
        slot = slot_at(k)
        hit = jnp.logical_and(lax.div(slot, sn_blocks) == owner, k < count)
        return (
            jnp.where(hit, k, which),
            jnp.where(hit, lax.rem(slot, sn_blocks), block),
            jnp.where(hit, 1.0, live),
        )

    start = (jnp.int32(0), jnp.int32(0), F32(0.0))
    return lax.fori_loop(0, targets, look, start, unroll=targets <= 8)


def low_lanes(shape):
    return lax.broadcasted_iota(jnp.int32, shape, 1) < BLOCK // 2


def swap_halves(upper, lower):
    low = low_lanes(upper.shape)
    half = BLOCK // 2
    return (
        jnp.where(low, upper, pltpu.roll(lower, half, 1)),
        jnp.where(low, pltpu.roll(upper, half, 1), lower),
    )


def columns_of(rows):
    padded = jnp.concatenate([rows, jnp.zeros((5, rows.shape[1]), F32)], axis=0)
    return jnp.transpose(padded)


def thirds(x):
    first = x.astype(BF16).astype(F32)
    second = (x - first).astype(BF16).astype(F32)
    third = x - first - second
    return [first, second, third]


def encoder_kernel(
    owners,
    n_sn,
    sn_blocks,
    targets,
    target_block_in,
    target_links_in,
    target_count_in,
    block_slot_in,
    feats_in,
    positions_in,
    sn_positions_in,
    w_in_in,
    w_mid_in,
    w_post_in,
    queries_in,
    w_key_in,
    w_value_in,
    features_out,
    landed,
    target_block,
    target_links,
    target_count,
    block_slot,
    points,
    positions,
    sn_positions,
    w_in,
    w_mid,
    w_post,
    queries,
    w_key,
    w_value,
    load_sem,
    pooled,
    features,
    values_t,
    keys,
    masked,
    peak_so_far,
    total_so_far,
    out_so_far,
    all_scores,
    all_probs,
    whole_features,
    parts,
    part_send,
    part_recv,
    pair_out,
    pair_in,
    pair_send,
    pair_recv,
    arrived_a,
    arrived_b,
    sums_a,
    sums_b,
    block_of,
    wanted,
    everywhere,
    hidden,
    point_blocks,
    outgoing_a,
    outgoing_b,
    slots,
    pos_send,
    pos_recv,
    msg_send_a,
    msg_recv_a,
    msg_send_b,
    msg_recv_b,
    own_sem,
):
    me = place(n_sn)
    links = target_links.shape[0]
    width = points.shape[0]
    loads = [
        pltpu.make_async_copy(source, target, load_sem.at[i])
        for i, (source, target) in enumerate(
            [
                (target_block_in, target_block),
                (block_slot_in, block_slot),
                (target_count_in, target_count),
                (target_links_in, target_links),
                (sn_positions_in, sn_positions),
                (feats_in, points),
                (w_in_in, w_in),
                (w_mid_in, w_mid),
                (positions_in, positions),
                (w_post_in, w_post),
                (w_key_in, w_key),
                (w_value_in, w_value),
                (queries_in, queries),
            ]
        )
    ]
    for load in loads[:5]:
        load.start()
    barrier = greet(owners, me, n_sn)
    for load in loads[5:]:
        load.start()
    for load in loads[:5]:
        load.wait()

    def choose(region, carry):
        def slot_at(k):
            return block_slot[target_block[region * targets + k]]

        block = named_block(me, targets, sn_blocks, target_count[region], slot_at)[1]
        block_of[region] = block
        rows = sn_positions[:, :BLOCK]
        for b in range(1, sn_blocks):
            rows = jnp.where(block == b, sn_positions[:, b * BLOCK : (b + 1) * BLOCK], rows)
        wanted[region] = rows
        return carry

    lax.fori_loop(0, owners, choose, 0, unroll=4)

    def slot_of(k, carry):
        slots[k] = block_slot[target_block[me * targets + k]]
        return carry

    lax.fori_loop(0, targets, slot_of, 0)
    my_count = target_count[me]

    def pos_copy(other, slot_at):
        return pltpu.make_async_remote_copy(
            src_ref=wanted.at[other],
            dst_ref=everywhere.at[slot_at],
            send_sem=pos_send.at[other],
            recv_sem=pos_recv.at[slot_at],
            device_id=peer(other, n_sn),
            device_id_type=MESH,
        )

    def start_pos(i, carry):
        pos_copy(across_first(me, i, owners), me).start()
        return carry

    def mlp(step, carry):
        span = pl.ds(pl.multiple_of(step * CHUNK, CHUNK), CHUNK)
        inner = jax.nn.gelu(contract(w_in[...], points[:, span], 0, 0)).astype(BF16)
        hid = contract(w_mid[...], inner, 0, 0).astype(BF16)
        places = positions[:, span]
        for q in range(CHUNK // BLOCK):
            hidden[step * (CHUNK // BLOCK) + q] = hid[:, q * BLOCK : (q + 1) * BLOCK]
            point_blocks[step * (CHUNK // BLOCK) + q] = places[:, q * BLOCK : (q + 1) * BLOCK]
        return carry

    mlp_steps = points.shape[1] // CHUNK
    for load in loads[5:9]:
        load.wait()
    early = early_steps(mlp_steps)
    lax.fori_loop(0, early, mlp, 0)
    pl.semaphore_wait(barrier, owners - 1)
    lax.fori_loop(0, owners - 1, start_pos, 0, unroll=owners <= 16)
    own_pos = pltpu.make_async_copy(wanted.at[me], everywhere.at[me], own_sem.at[0])
    own_pos.start()
    lax.fori_loop(early, mlp_steps, mlp, 0)
    for load in loads[9:]:
        load.wait()

    outgoing = (outgoing_a, outgoing_b)
    arrived = (arrived_a, arrived_b)
    sums = (sums_a, sums_b)
    msg_send = (msg_send_a, msg_send_b)
    msg_recv = (msg_recv_a, msg_recv_b)
    half_rows = width // 2

    def msg_copy(p, other, slot_at):
        return pltpu.make_async_remote_copy(
            src_ref=outgoing[p].at[other],
            dst_ref=arrived[p].at[slot_at],
            send_sem=msg_send[p].at[other],
            recv_sem=msg_recv[p].at[slot_at],
            device_id=peer(other, n_sn),
            device_id_type=MESH,
        )

    def build(other):
        which, block, live = named_block(
            other, targets, sn_blocks, my_count, lambda k: slots[k]
        )
        sn_cols = columns_of(everywhere[other])
        kernels = []
        blocks = []
        for j in range(links):
            link = target_links[j, which]
            pts = point_blocks[link]
            dist = jnp.zeros((BLOCK, BLOCK), F32)
            for c in range(3):
                gap = sn_cols[:, c : c + 1] - pts[c : c + 1, :]
                dist = dist + gap * gap
            kernels.append(1.0 / (1.0 + dist * INV_RADIUS_SQ))
            blocks.append(hidden[link])
        total = kernels[0]
        for extra in kernels[1:]:
            total = total + extra
        total = jnp.sum(jnp.transpose(total), axis=0, keepdims=True)
        message = contract(
            jnp.concatenate(blocks, axis=1),
            jnp.concatenate([one.astype(BF16) for one in kernels], axis=1),
            1,
            1,
        )
        message = message * live
        halves = swap_halves(message[:half_rows], message[half_rows:])
        return (
            halves[0].astype(BF16),
            halves[1].astype(BF16),
            jnp.broadcast_to(total * live, (STAT_ROWS, BLOCK)).astype(BF16),
        )

    def nth(i):
        return across_first(me, i, owners)

    def build_next(i, carry):
        other = nth(i)
        pos_copy(other, other).wait_recv()
        first_half, second_half, total = build(other)
        outgoing_a[other, :half_rows, :] = first_half
        outgoing_a[other, half_rows:, :] = total
        outgoing_b[other] = second_half
        msg_copy(0, other, me).start()
        return carry

    lax.fori_loop(0, owners - 1, build_next, 0)

    def send_second(i, carry):
        msg_copy(1, nth(i), me).start()
        return carry

    lax.fori_loop(0, owners - 1, send_second, 0)
    own_pos.wait()
    own_first, own_second, own_total = build(me)
    outgoing_a[me, :half_rows, :] = own_first
    outgoing_a[me, half_rows:, :] = own_total
    outgoing_b[me] = own_second

    def source_of(n):
        return lax.rem(me + n, owners)

    def gather(p):
        sums[p][...] = jnp.zeros(sums[p].shape, F32)

        def add(source, message):
            block = block_of[source]
            for b in range(sn_blocks):
                sums[p][b] += jnp.where(block == b, message, 0.0)

        add(me, outgoing[p][me].astype(F32))

        def arrive(n, carry):
            source = source_of(n)
            msg_copy(p, source, source).wait_recv()
            add(source, arrived[p][source].astype(F32))
            return carry

        lax.fori_loop(1, owners, arrive, 0)

    def pool(p):
        for pair in range(sn_blocks // 2):
            scaled = []
            for b in (2 * pair, 2 * pair + 1):
                total = sums_a[b][half_rows : half_rows + 1, :]
                scale = 1.0 / (1.0 + total)
                scale = swap_halves(scale, scale)[p]
                scaled.append(sums[p][b][:half_rows, :] * scale)
            upper, lower = swap_halves(scaled[0], scaled[1])
            columns = slice(pair * BLOCK, (pair + 1) * BLOCK)
            pooled[:half_rows, columns] = upper.astype(BF16)
            pooled[half_rows:, columns] = lower.astype(BF16)

    head_width = width // HEADS
    latents = queries.shape[1]
    share = latents // owners
    group = latents // 2
    piece = group // n_sn
    places = owners // n_sn
    my_pts = lax.axis_index("pts")
    my_sn = lax.axis_index("sn")
    row_head = lax.broadcasted_iota(jnp.int32, queries.shape, 0) // head_width
    column = lax.broadcasted_iota(jnp.int32, (latents, latents), 1)
    inside = column % piece
    place_of = column // group * (places // 2) + inside // share
    taken = (place_of * n_sn + column % group // piece) * share + inside % share
    pick = lax.broadcasted_iota(jnp.int32, (latents, latents), 0) == taken
    by_core = contract(queries[...], jnp.where(pick, 1.0, 0.0).astype(BF16), 1, 0).astype(BF16)
    scaled_queries = by_core * BF16(head_width ** (-0.5))
    for h in range(HEADS):
        masked[h] = jnp.where(row_head == h, scaled_queries, BF16(0.0))

    def project(p):
        pool(p)
        features[p] = jax.nn.gelu(contract(w_post[...], pooled[...], 0, 0)).astype(BF16)
        keys[...] = contract(features[p], w_key[...], 0, 0).astype(BF16)
        values_t[...] = contract(w_value[...], features[p], 0, 0).astype(BF16)

    def head_rows(h):
        return slice(h * head_width, (h + 1) * head_width)

    def score():
        for side in range(2):
            lanes = slice(side * group, (side + 1) * group)
            for h in range(HEADS):
                all_scores[h, :, lanes] = contract(keys[...], masked[h, :, lanes], 1, 0)

    def weigh(h, lanes):
        return contract(values_t[head_rows(h), :], all_probs[h, :, lanes], 1, 0)

    gather(0)
    project(0)
    score()
    for h in range(HEADS):
        for at in range(0, latents, piece):
            lanes = slice(at, at + piece)
            scores = all_scores[h, :, lanes]
            peak = jnp.max(scores, axis=0, keepdims=True)
            probs = jnp.exp(scores - peak)
            peak_so_far[h : h + 1, lanes] = peak
            total_so_far[h : h + 1, lanes] = jnp.sum(probs, axis=0, keepdims=True)
            all_probs[h, :, lanes] = probs.astype(BF16)
    for side in range(2):
        lanes = slice(side * group, (side + 1) * group)
        for h in range(HEADS):
            out_so_far[head_rows(h), lanes] = weigh(h, lanes)
    gather(1)
    project(1)

    def attend(side, core):
        lanes = pl.ds(pl.multiple_of(side * group + core * piece, piece), piece)
        kept = []
        for h in range(HEADS):
            scores = all_scores[h, :, lanes]
            old_peak = peak_so_far[h : h + 1, lanes]
            peak = jnp.maximum(old_peak, jnp.max(scores, axis=0, keepdims=True))
            shrink = jnp.exp(old_peak - peak)
            probs = jnp.exp(scores - peak)
            total = jnp.sum(probs, axis=0, keepdims=True)
            all_probs[h, :, lanes] = probs.astype(BF16)
            kept.append((peak, total + shrink * total_so_far[h : h + 1, lanes], shrink))
        state = []
        for h, (peak, total, shrink) in enumerate(kept):
            out = weigh(h, lanes) + shrink * out_so_far[head_rows(h), lanes]
            state.append((peak, total, out))
        return state

    def pair_copy(side):
        return pltpu.make_async_remote_copy(
            src_ref=pair_out.at[side],
            dst_ref=pair_in.at[side],
            send_sem=pair_send.at[side],
            recv_sem=pair_recv.at[side],
            device_id={"pts": my_pts, "sn": 1 - my_sn},
            device_id_type=MESH,
        )

    def copy_of(other, slot_at):
        return pltpu.make_async_remote_copy(
            src_ref=parts.at[other],
            dst_ref=landed.at[slot_at],
            send_sem=part_send.at[other],
            recv_sem=part_recv.at[slot_at],
            device_id={"pts": other, "sn": my_sn},
            device_id_type=MESH,
        )

    def hand_over(side):
        for h, (peak, total, out) in enumerate(attend(side, 1 - my_sn)):
            pair_out[side, head_rows(h), :] = out
            pair_out[side, width + h : width + h + 1, :] = peak
            pair_out[side, width + HEADS + h : width + HEADS + h + 1, :] = total
        pair_out[side, width + 2 * HEADS :, :] = jnp.zeros((8 - 2 * HEADS, piece), F32)
        pair_copy(side).start()

    def merge(side, mine):
        pair_copy(side).wait_recv()
        outs, peaks, totals = [], [], []
        for h, (peak, total, out) in enumerate(mine):
            their_peak = pair_in[side, width + h : width + h + 1, :]
            their_total = pair_in[side, width + HEADS + h : width + HEADS + h + 1, :]
            top = jnp.maximum(peak, their_peak)
            shrink = jnp.exp(peak - top)
            their_shrink = jnp.exp(their_peak - top)
            peaks += thirds(top)
            totals += thirds(total * shrink + their_total * their_shrink)
            outs.append(out * shrink + pair_in[side, head_rows(h), :] * their_shrink)
        pad = jnp.zeros((OUT_LANES - width - 6 * HEADS, piece), F32)
        merged = jnp.concatenate(outs + peaks + totals + [pad], axis=0)
        merged = jnp.transpose(merged.astype(BF16))
        first_place = side * (places // 2)
        for j in range(places // 2):
            parts[first_place + j] = merged[j * share : (j + 1) * share, :]

        def send_part(j, carry):
            other = first_place + j

            @pl.when(other != my_pts)
            def _():
                copy_of(other, my_pts).start()

            return carry

        lax.fori_loop(0, places // 2, send_part, 0, unroll=places <= 8)

    score()
    hand_over(0)
    near = attend(0, my_sn)
    hand_over(1)
    merge(0, near)
    merge(1, attend(1, my_sn))
    own = pltpu.make_async_copy(parts.at[my_pts], landed.at[my_pts], own_sem.at[1])
    own.start()
    for pair in range(sn_blocks // 2):
        columns = slice(pair * BLOCK, (pair + 1) * BLOCK)
        whole = swap_halves(features[0, :, columns].astype(F32), features[1, :, columns].astype(F32))
        for side in range(2):
            at = (2 * pair + side) * BLOCK
            whole_features[:, at : at + BLOCK] = whole[side].astype(BF16)
    store = pltpu.make_async_copy(whole_features, features_out, own_sem.at[2])
    store.start()

    def sent(i, carry):
        msg_copy(0, nth(i), nth(i)).wait_send()
        msg_copy(1, nth(i), nth(i)).wait_send()
        pos_copy(nth(i), nth(i)).wait_send()
        return carry

    lax.fori_loop(0, owners - 1, sent, 0)
    pair_copy(0).wait_send()
    pair_copy(1).wait_send()
    own.wait()

    def settle(off, carry):
        other = lax.rem(my_pts + off, places)
        copy = copy_of(other, other)
        copy.wait_send()
        copy.wait_recv()
        return carry

    lax.fori_loop(1, places, settle, 0)
    store.wait()


def finish_kernel(features_in, landed, w_out, out_gain, features, latent_out, sem):
    move = pltpu.make_async_copy(features_in, features, sem)
    move.start()
    owners, share, _ = landed.shape
    width = w_out.shape[0]
    head_width = width // HEADS
    lane = lax.broadcasted_iota(jnp.int32, (OUT_LANES, width), 0) - width
    head_of = lax.broadcasted_iota(jnp.int32, (OUT_LANES, width), 1) // head_width
    is_peak = jnp.logical_and(lane >= 3 * head_of, lane < 3 * head_of + 3)
    total_lane = lane - 3 * HEADS
    is_total = jnp.logical_and(total_lane >= 3 * head_of, total_lane < 3 * head_of + 3)
    flat = jnp.concatenate([landed[source] for source in range(owners)], axis=0)
    peaks = contract(flat, jnp.where(is_peak, 1.0, 0.0).astype(BF16), 1, 0)
    totals = contract(flat, jnp.where(is_total, 1.0, 0.0).astype(BF16), 1, 0)

    def of(full, source):
        return full[source * share : (source + 1) * share, :]

    top = of(peaks, 0)
    for source in range(1, owners):
        top = jnp.maximum(top, of(peaks, source))
    output = jnp.zeros((share, width), F32)
    total = jnp.zeros((share, width), F32)
    for source in range(owners):
        scale = jnp.exp(of(peaks, source) - top)
        output = output + scale * landed[source][:, :width].astype(F32)
        total = total + scale * of(totals, source)
    attended = (output / total).astype(BF16)
    projected = jnp.dot(attended, w_out[...], preferred_element_type=F32)
    mean_sq = jnp.mean(projected * projected, axis=-1, keepdims=True)
    normed = projected * lax.rsqrt(mean_sq + 1e-06)
    latent_out[...] = (normed * out_gain[...]).astype(BF16)
    move.wait()


def per_device(
    n_sn,
    owners,
    point_features,
    point_positions,
    sn_positions,
    latent_queries,
    target_block,
    target_links,
    target_count,
    block_slot,
    w_in,
    w_mid,
    w_post,
    w_key,
    w_value,
    w_out,
    out_gain,
):
    targets = target_links.shape[0]
    width = point_features.shape[1]
    sn_rows = sn_positions.shape[1]
    sn_blocks = sn_rows // BLOCK
    latents = latent_queries.shape[0]
    share = latents // owners
    vmem = pl.BlockSpec(memory_space=pltpu.VMEM)
    hbm = pl.BlockSpec(memory_space=pl.ANY)
    dma = pltpu.SemaphoreType.DMA
    points = point_features.shape[0]
    rows_a = width // 2 + STAT_ROWS
    features_t, landed = pl.pallas_call(
        functools.partial(encoder_kernel, owners, n_sn, sn_blocks, targets),
        out_shape=(
            jax.ShapeDtypeStruct((width, sn_rows), BF16),
            jax.ShapeDtypeStruct((owners // n_sn, share, OUT_LANES), BF16),
        ),
        in_specs=[hbm] * 13,
        out_specs=(hbm, hbm),
        scratch_shapes=[
            pltpu.SMEM(target_block.shape, jnp.int32),
            pltpu.SMEM(target_links.shape[::-1], jnp.int32),
            pltpu.SMEM(target_count.shape, jnp.int32),
            pltpu.SMEM(block_slot.shape, jnp.int32),
            pltpu.VMEM((width, points), BF16),
            pltpu.VMEM(point_positions.shape, F32),
            pltpu.VMEM(sn_positions.shape, F32),
            pltpu.VMEM(w_in.shape, BF16),
            pltpu.VMEM(w_mid.shape, BF16),
            pltpu.VMEM(w_post.shape, BF16),
            pltpu.VMEM(latent_queries.shape[::-1], BF16),
            pltpu.VMEM(w_key.shape, BF16),
            pltpu.VMEM(w_value.shape, BF16),
            dma((13,)),
            pltpu.VMEM((width, sn_rows // 2), BF16),
            pltpu.VMEM((2, width, sn_rows // 2), BF16),
            pltpu.VMEM((width, sn_rows // 2), BF16),
            pltpu.VMEM((sn_rows // 2, width), BF16),
            pltpu.VMEM((HEADS, width, latents), BF16),
            pltpu.VMEM((HEADS, latents), F32),
            pltpu.VMEM((HEADS, latents), F32),
            pltpu.VMEM((width, latents), F32),
            pltpu.VMEM((HEADS, sn_rows // 2, latents), F32),
            pltpu.VMEM((HEADS, sn_rows // 2, latents), BF16),
            pltpu.VMEM((width, sn_rows), BF16),
            pltpu.VMEM((owners // n_sn, share, OUT_LANES), BF16),
            dma((owners // n_sn,)),
            dma((owners // n_sn,)),
            pltpu.VMEM((2, width + 8, latents // (2 * n_sn)), F32),
            pltpu.VMEM((2, width + 8, latents // (2 * n_sn)), F32),
            dma((2,)),
            dma((2,)),
            pltpu.VMEM((owners, rows_a, BLOCK), BF16),
            pltpu.VMEM((owners, width // 2, BLOCK), BF16),
            pltpu.VMEM((sn_blocks, rows_a, BLOCK), F32),
            pltpu.VMEM((sn_blocks, width // 2, BLOCK), F32),
            pltpu.SMEM((owners,), jnp.int32),
            pltpu.VMEM((owners, 3, BLOCK), F32),
            pltpu.VMEM((owners, 3, BLOCK), F32),
            pltpu.VMEM((points // BLOCK, width, BLOCK), BF16),
            pltpu.VMEM((points // BLOCK, 3, BLOCK), F32),
            pltpu.VMEM((owners, rows_a, BLOCK), BF16),
            pltpu.VMEM((owners, width // 2, BLOCK), BF16),
            pltpu.SMEM((targets,), jnp.int32),
            dma((owners,)),
            dma((owners,)),
            dma((owners,)),
            dma((owners,)),
            dma((owners,)),
            dma((owners,)),
            dma((3,)),
        ],
        compiler_params=pltpu.CompilerParams(
            collective_id=0, has_side_effects=True, vmem_limit_bytes=VMEM_LIMIT
        ),
        name="encoder",
    )(
        *(
            pltpu.with_memory_space_constraint(operand, pltpu.HBM)
            for operand in (
                target_block,
                target_links.T,
                target_count,
                block_slot,
                point_features.T,
                point_positions,
                sn_positions,
                w_in,
                w_mid,
                w_post,
                latent_queries.T,
                w_key,
                w_value,
            )
        )
    )
    features_t, latent_out = pl.pallas_call(
        finish_kernel,
        out_shape=(
            jax.ShapeDtypeStruct((width, sn_rows), BF16),
            jax.ShapeDtypeStruct((share, width), BF16),
        ),
        in_specs=[hbm] + [vmem] * 3,
        out_specs=(hbm, vmem),
        scratch_shapes=[dma],
        compiler_params=pltpu.CompilerParams(vmem_limit_bytes=VMEM_LIMIT),
        name="finish",
    )(features_t, landed, w_out, out_gain.reshape(1, width))
    return (features_t.T, latent_out)


def solution(mesh):
    n_sn = mesh.shape["sn"]
    owners = mesh.shape["pts"] * n_sn
    everything = ("groups", "pts", "sn")
    in_specs = (
        P(everything, None),
        P(None, everything),
        P(None, everything),
        P(),
        P("groups"),
        P(everything, None),
        P("groups"),
        P("groups"),
        P(),
        P(),
        P(),
        P(),
        P(),
        P(),
        P(),
    )
    out_specs = (P(everything, None), P(everything, None))
    return jax.shard_map(
        functools.partial(per_device, n_sn, owners),
        mesh=mesh,
        in_specs=in_specs,
        out_specs=out_specs,
        check_vma=False,
    )
```

```python
import functools

import jax
import jax.numpy as jnp
from jax import lax
from jax.experimental import pallas as pl
from jax.experimental.pallas import tpu as pltpu
from jax.sharding import PartitionSpec as P

HEADS = 3
BLOCK = 128
INV_RADIUS_SQ = 100.0
MESH = pl.DeviceIdType.MESH
STAT_ROWS = 8
CHUNK = 2048
OUT_LANES = 256
VMEM_LIMIT = 40 * 2**20
F32 = jnp.float32
BF16 = jnp.bfloat16


def contract(a, b, dim_a, dim_b):
    return lax.dot_general(a, b, (((dim_a,), (dim_b,)), ((), ())), preferred_element_type=F32)


def place(n_sn):
    return lax.axis_index("pts") * n_sn + lax.axis_index("sn")


def peer(index, n_sn):
    return {"pts": lax.div(index, n_sn), "sn": lax.rem(index, n_sn)}


def greet(owners, me, n_sn):
    barrier = pltpu.get_barrier_semaphore()

    def signal(i, carry):
        other = across_first(me, i, owners)
        pl.semaphore_signal(barrier, inc=1, device_id=peer(other, n_sn), device_id_type=MESH)
        return carry

    lax.fori_loop(0, owners - 1, signal, 0, unroll=owners <= 16)
    return barrier


def early_steps(steps):
    left = 3 - lax.div(lax.axis_index("pts") * 4, lax.axis_size("pts"))
    return steps // 2 * lax.div(left * left, 4)


def across_first(me, i, owners):
    left = owners - 1 - i
    top = 1
    bit = 2
    while bit < owners:
        top = jnp.where(left >= bit, bit, top)
        bit *= 2
    offset = 3 * top - 1 - left
    other = 0
    bit = 1
    while bit < owners:
        other = other + bit * lax.rem(lax.div(me, bit) + lax.div(offset, bit), 2)
        bit *= 2
    return other


def named_block(owner, targets, sn_blocks, count, slot_at):
    def look(k, state):
        which, block, live = state
        slot = slot_at(k)
        hit = jnp.logical_and(lax.div(slot, sn_blocks) == owner, k < count)
        return (
            jnp.where(hit, k, which),
            jnp.where(hit, lax.rem(slot, sn_blocks), block),
            jnp.where(hit, 1.0, live),
        )

    start = (jnp.int32(0), jnp.int32(0), F32(0.0))
    return lax.fori_loop(0, targets, look, start, unroll=targets <= 8)


def low_lanes(shape):
    return lax.broadcasted_iota(jnp.int32, shape, 1) < BLOCK // 2


def swap_halves(upper, lower):
    low = low_lanes(upper.shape)
    half = BLOCK // 2
    return (
        jnp.where(low, upper, pltpu.roll(lower, half, 1)),
        jnp.where(low, pltpu.roll(upper, half, 1), lower),
    )


def columns_of(rows):
    padded = jnp.concatenate([rows, jnp.zeros((5, rows.shape[1]), F32)], axis=0)
    return jnp.transpose(padded)


def thirds(x):
    first = x.astype(BF16).astype(F32)
    second = (x - first).astype(BF16).astype(F32)
    third = x - first - second
    return [first, second, third]


def encoder_kernel(
    owners,
    n_sn,
    sn_blocks,
    targets,
    target_block_in,
    target_links_in,
    target_count_in,
    block_slot_in,
    feats_in,
    positions_in,
    sn_positions_in,
    w_in_in,
    w_mid_in,
    w_post_in,
    queries_in,
    w_key_in,
    w_value_in,
    features_out,
    landed,
    target_block,
    target_links,
    target_count,
    block_slot,
    points,
    positions,
    sn_positions,
    w_in,
    w_mid,
    w_post,
    queries,
    w_key,
    w_value,
    load_sem,
    pooled,
    features,
    values_t,
    keys,
    masked,
    peak_so_far,
    total_so_far,
    out_so_far,
    all_scores,
    all_probs,
    whole_features,
    parts,
    part_send,
    part_recv,
    pair_out,
    pair_in,
    pair_send,
    pair_recv,
    arrived_a,
    arrived_b,
    sums_a,
    sums_b,
    block_of,
    wanted,
    everywhere,
    hidden,
    point_blocks,
    outgoing_a,
    outgoing_b,
    slots,
    pos_send,
    pos_recv,
    msg_send_a,
    msg_recv_a,
    msg_send_b,
    msg_recv_b,
    own_sem,
):
    me = place(n_sn)
    links = target_links.shape[0]
    width = points.shape[0]
    loads = [
        pltpu.make_async_copy(source, target, load_sem.at[i])
        for i, (source, target) in enumerate(
            [
                (target_block_in, target_block),
                (block_slot_in, block_slot),
                (target_count_in, target_count),
                (target_links_in, target_links),
                (sn_positions_in, sn_positions),
                (feats_in, points),
                (w_in_in, w_in),
                (w_mid_in, w_mid),
                (positions_in, positions),
                (w_post_in, w_post),
                (w_key_in, w_key),
                (w_value_in, w_value),
                (queries_in, queries),
            ]
        )
    ]
    for load in loads[:5]:
        load.start()
    barrier = greet(owners, me, n_sn)
    for load in loads[5:]:
        load.start()
    for load in loads[:5]:
        load.wait()

    def choose(region, carry):
        def slot_at(k):
            return block_slot[target_block[region * targets + k]]

        block = named_block(me, targets, sn_blocks, target_count[region], slot_at)[1]
        block_of[region] = block
        rows = sn_positions[:, :BLOCK]
        for b in range(1, sn_blocks):
            rows = jnp.where(block == b, sn_positions[:, b * BLOCK : (b + 1) * BLOCK], rows)
        wanted[region] = rows
        return carry

    lax.fori_loop(0, owners, choose, 0, unroll=4)

    def slot_of(k, carry):
        slots[k] = block_slot[target_block[me * targets + k]]
        return carry

    lax.fori_loop(0, targets, slot_of, 0)
    my_count = target_count[me]

    def pos_copy(other, slot_at):
        return pltpu.make_async_remote_copy(
            src_ref=wanted.at[other],
            dst_ref=everywhere.at[slot_at],
            send_sem=pos_send.at[other],
            recv_sem=pos_recv.at[slot_at],
            device_id=peer(other, n_sn),
            device_id_type=MESH,
        )

    def start_pos(i, carry):
        pos_copy(across_first(me, i, owners), me).start()
        return carry

    def mlp(step, carry):
        span = pl.ds(pl.multiple_of(step * CHUNK, CHUNK), CHUNK)
        inner = jax.nn.gelu(contract(w_in[...], points[:, span], 0, 0)).astype(BF16)
        hid = contract(w_mid[...], inner, 0, 0).astype(BF16)
        places = positions[:, span]
        for q in range(CHUNK // BLOCK):
            hidden[step * (CHUNK // BLOCK) + q] = hid[:, q * BLOCK : (q + 1) * BLOCK]
            point_blocks[step * (CHUNK // BLOCK) + q] = places[:, q * BLOCK : (q + 1) * BLOCK]
        return carry

    mlp_steps = points.shape[1] // CHUNK
    for load in loads[5:9]:
        load.wait()
    early = early_steps(mlp_steps)
    lax.fori_loop(0, early, mlp, 0)
    pl.semaphore_wait(barrier, owners - 1)
    lax.fori_loop(0, owners - 1, start_pos, 0, unroll=owners <= 16)
    own_pos = pltpu.make_async_copy(wanted.at[me], everywhere.at[me], own_sem.at[0])
    own_pos.start()
    lax.fori_loop(early, mlp_steps, mlp, 0)
    for load in loads[9:]:
        load.wait()

    outgoing = (outgoing_a, outgoing_b)
    arrived = (arrived_a, arrived_b)
    sums = (sums_a, sums_b)
    msg_send = (msg_send_a, msg_send_b)
    msg_recv = (msg_recv_a, msg_recv_b)
    half_rows = width // 2

    def msg_copy(p, other, slot_at):
        return pltpu.make_async_remote_copy(
            src_ref=outgoing[p].at[other],
            dst_ref=arrived[p].at[slot_at],
            send_sem=msg_send[p].at[other],
            recv_sem=msg_recv[p].at[slot_at],
            device_id=peer(other, n_sn),
            device_id_type=MESH,
        )

    def build(other):
        which, block, live = named_block(
            other, targets, sn_blocks, my_count, lambda k: slots[k]
        )
        sn_cols = columns_of(everywhere[other])
        kernels = []
        blocks = []
        for j in range(links):
            link = target_links[j, which]
            pts = point_blocks[link]
            dist = jnp.zeros((BLOCK, BLOCK), F32)
            for c in range(3):
                gap = sn_cols[:, c : c + 1] - pts[c : c + 1, :]
                dist = dist + gap * gap
            kernels.append(1.0 / (1.0 + dist * INV_RADIUS_SQ))
            blocks.append(hidden[link])
        total = kernels[0]
        for extra in kernels[1:]:
            total = total + extra
        total = jnp.sum(jnp.transpose(total), axis=0, keepdims=True)
        message = contract(
            jnp.concatenate(blocks, axis=1),
            jnp.concatenate([one.astype(BF16) for one in kernels], axis=1),
            1,
            1,
        )
        message = message * live
        halves = swap_halves(message[:half_rows], message[half_rows:])
        return (
            halves[0].astype(BF16),
            halves[1].astype(BF16),
            jnp.broadcast_to(total * live, (STAT_ROWS, BLOCK)).astype(BF16),
        )

    def nth(i):
        return across_first(me, i, owners)

    def build_next(i, carry):
        other = nth(i)
        pos_copy(other, other).wait_recv()
        first_half, second_half, total = build(other)
        outgoing_a[other, :half_rows, :] = first_half
        outgoing_a[other, half_rows:, :] = total
        outgoing_b[other] = second_half
        msg_copy(0, other, me).start()
        return carry

    lax.fori_loop(0, owners - 1, build_next, 0)

    def send_second(i, carry):
        msg_copy(1, nth(i), me).start()
        return carry

    lax.fori_loop(0, owners - 1, send_second, 0)
    own_pos.wait()
    own_first, own_second, own_total = build(me)
    outgoing_a[me, :half_rows, :] = own_first
    outgoing_a[me, half_rows:, :] = own_total
    outgoing_b[me] = own_second

    def source_of(n):
        return lax.rem(me + n, owners)

    def gather(p):
        sums[p][...] = jnp.zeros(sums[p].shape, F32)

        def add(source, message):
            block = block_of[source]
            for b in range(sn_blocks):
                sums[p][b] += jnp.where(block == b, message, 0.0)

        add(me, outgoing[p][me].astype(F32))

        def arrive(n, carry):
            source = source_of(n)
            msg_copy(p, source, source).wait_recv()
            add(source, arrived[p][source].astype(F32))
            return carry

        lax.fori_loop(1, owners, arrive, 0)

    def pool(p):
        for pair in range(sn_blocks // 2):
            scaled = []
            for b in (2 * pair, 2 * pair + 1):
                total = sums_a[b][half_rows : half_rows + 1, :]
                scale = 1.0 / (1.0 + total)
                scale = swap_halves(scale, scale)[p]
                scaled.append(sums[p][b][:half_rows, :] * scale)
            upper, lower = swap_halves(scaled[0], scaled[1])
            columns = slice(pair * BLOCK, (pair + 1) * BLOCK)
            pooled[:half_rows, columns] = upper.astype(BF16)
            pooled[half_rows:, columns] = lower.astype(BF16)

    head_width = width // HEADS
    latents = queries.shape[1]
    share = latents // owners
    group = latents // 2
    piece = group // n_sn
    places = owners // n_sn
    my_pts = lax.axis_index("pts")
    my_sn = lax.axis_index("sn")
    row_head = lax.broadcasted_iota(jnp.int32, queries.shape, 0) // head_width
    column = lax.broadcasted_iota(jnp.int32, (latents, latents), 1)
    inside = column % piece
    place_of = column // group * (places // 2) + inside // share
    taken = (place_of * n_sn + column % group // piece) * share + inside % share
    pick = lax.broadcasted_iota(jnp.int32, (latents, latents), 0) == taken
    by_core = contract(queries[...], jnp.where(pick, 1.0, 0.0).astype(BF16), 1, 0).astype(BF16)
    scaled_queries = by_core * BF16(head_width ** (-0.5))
    for h in range(HEADS):
        masked[h] = jnp.where(row_head == h, scaled_queries, BF16(0.0))

    def project(p):
        pool(p)
        features[p] = jax.nn.gelu(contract(w_post[...], pooled[...], 0, 0)).astype(BF16)
        keys[...] = contract(features[p], w_key[...], 0, 0).astype(BF16)
        values_t[...] = contract(w_value[...], features[p], 0, 0).astype(BF16)

    def head_rows(h):
        return slice(h * head_width, (h + 1) * head_width)

    def score():
        for side in range(2):
            lanes = slice(side * group, (side + 1) * group)
            for h in range(HEADS):
                all_scores[h, :, lanes] = contract(keys[...], masked[h, :, lanes], 1, 0)

    def weigh(h, lanes):
        return contract(values_t[head_rows(h), :], all_probs[h, :, lanes], 1, 0)

    gather(0)
    project(0)
    score()
    for h in range(HEADS):
        for at in range(0, latents, piece):
            lanes = slice(at, at + piece)
            scores = all_scores[h, :, lanes]
            peak = jnp.max(scores, axis=0, keepdims=True)
            probs = jnp.exp(scores - peak)
            peak_so_far[h : h + 1, lanes] = peak
            total_so_far[h : h + 1, lanes] = jnp.sum(probs, axis=0, keepdims=True)
            all_probs[h, :, lanes] = probs.astype(BF16)
    for side in range(2):
        lanes = slice(side * group, (side + 1) * group)
        for h in range(HEADS):
            out_so_far[head_rows(h), lanes] = weigh(h, lanes)
    def sent_first(i, carry):
        msg_copy(0, nth(i), nth(i)).wait_send()
        pos_copy(nth(i), nth(i)).wait_send()
        return carry

    lax.fori_loop(0, owners - 1, sent_first, 0)
    gather(1)
    project(1)

    def attend(side, core):
        lanes = pl.ds(pl.multiple_of(side * group + core * piece, piece), piece)
        kept = []
        for h in range(HEADS):
            scores = all_scores[h, :, lanes]
            old_peak = peak_so_far[h : h + 1, lanes]
            peak = jnp.maximum(old_peak, jnp.max(scores, axis=0, keepdims=True))
            shrink = jnp.exp(old_peak - peak)
            probs = jnp.exp(scores - peak)
            total = jnp.sum(probs, axis=0, keepdims=True)
            all_probs[h, :, lanes] = probs.astype(BF16)
            kept.append((peak, total + shrink * total_so_far[h : h + 1, lanes], shrink))
        state = []
        for h, (peak, total, shrink) in enumerate(kept):
            out = weigh(h, lanes) + shrink * out_so_far[head_rows(h), lanes]
            state.append((peak, total, out))
        return state

    def pair_copy(side):
        return pltpu.make_async_remote_copy(
            src_ref=pair_out.at[side],
            dst_ref=pair_in.at[side],
            send_sem=pair_send.at[side],
            recv_sem=pair_recv.at[side],
            device_id={"pts": my_pts, "sn": 1 - my_sn},
            device_id_type=MESH,
        )

    def copy_of(other, slot_at):
        return pltpu.make_async_remote_copy(
            src_ref=parts.at[other],
            dst_ref=landed.at[slot_at],
            send_sem=part_send.at[other],
            recv_sem=part_recv.at[slot_at],
            device_id={"pts": other, "sn": my_sn},
            device_id_type=MESH,
        )

    def hand_over(side):
        for h, (peak, total, out) in enumerate(attend(side, 1 - my_sn)):
            pair_out[side, head_rows(h), :] = out
            pair_out[side, width + h : width + h + 1, :] = peak
            pair_out[side, width + HEADS + h : width + HEADS + h + 1, :] = total
        pair_out[side, width + 2 * HEADS :, :] = jnp.zeros((8 - 2 * HEADS, piece), F32)
        pair_copy(side).start()

    def merge(side, mine):
        pair_copy(side).wait_recv()
        outs, peaks, totals = [], [], []
        for h, (peak, total, out) in enumerate(mine):
            their_peak = pair_in[side, width + h : width + h + 1, :]
            their_total = pair_in[side, width + HEADS + h : width + HEADS + h + 1, :]
            top = jnp.maximum(peak, their_peak)
            shrink = jnp.exp(peak - top)
            their_shrink = jnp.exp(their_peak - top)
            peaks += thirds(top)
            totals += thirds(total * shrink + their_total * their_shrink)
            outs.append(out * shrink + pair_in[side, head_rows(h), :] * their_shrink)
        pad = jnp.zeros((OUT_LANES - width - 6 * HEADS, piece), F32)
        merged = jnp.concatenate(outs + peaks + totals + [pad], axis=0)
        merged = jnp.transpose(merged.astype(BF16))
        first_place = side * (places // 2)
        for j in range(places // 2):
            parts[first_place + j] = merged[j * share : (j + 1) * share, :]

        def send_part(j, carry):
            other = first_place + j

            @pl.when(other != my_pts)
            def _():
                copy_of(other, my_pts).start()

            return carry

        lax.fori_loop(0, places // 2, send_part, 0, unroll=places <= 8)

    score()
    hand_over(0)
    near = attend(0, my_sn)
    hand_over(1)
    merge(0, near)
    merge(1, attend(1, my_sn))
    own = pltpu.make_async_copy(parts.at[my_pts], landed.at[my_pts], own_sem.at[1])
    own.start()
    for pair in range(sn_blocks // 2):
        columns = slice(pair * BLOCK, (pair + 1) * BLOCK)
        whole = swap_halves(features[0, :, columns].astype(F32), features[1, :, columns].astype(F32))
        for side in range(2):
            at = (2 * pair + side) * BLOCK
            whole_features[:, at : at + BLOCK] = whole[side].astype(BF16)
    store = pltpu.make_async_copy(whole_features, features_out, own_sem.at[2])
    store.start()

    def sent(i, carry):
        msg_copy(1, nth(i), nth(i)).wait_send()
        return carry

    lax.fori_loop(0, owners - 1, sent, 0)
    pair_copy(0).wait_send()
    pair_copy(1).wait_send()
    own.wait()

    def settle(off, carry):
        other = lax.rem(my_pts + off, places)
        copy = copy_of(other, other)
        copy.wait_send()
        copy.wait_recv()
        return carry

    lax.fori_loop(1, places, settle, 0)
    store.wait()


def finish_kernel(features_in, landed, w_out, out_gain, features, latents, latent_out, sem):
    move = pltpu.make_async_copy(features_in, features, sem.at[0])
    move.start()
    owners, share, _ = landed.shape
    width = w_out.shape[0]
    head_width = width // HEADS
    lane = lax.broadcasted_iota(jnp.int32, (OUT_LANES, width), 0) - width
    head_of = lax.broadcasted_iota(jnp.int32, (OUT_LANES, width), 1) // head_width
    is_peak = jnp.logical_and(lane >= 3 * head_of, lane < 3 * head_of + 3)
    total_lane = lane - 3 * HEADS
    is_total = jnp.logical_and(total_lane >= 3 * head_of, total_lane < 3 * head_of + 3)
    flat = jnp.concatenate([landed[source] for source in range(owners)], axis=0)
    peaks = contract(flat, jnp.where(is_peak, 1.0, 0.0).astype(BF16), 1, 0)
    totals = contract(flat, jnp.where(is_total, 1.0, 0.0).astype(BF16), 1, 0)

    def of(full, source):
        return full[source * share : (source + 1) * share, :]

    top = of(peaks, 0)
    for source in range(1, owners):
        top = jnp.maximum(top, of(peaks, source))
    output = jnp.zeros((share, width), F32)
    total = jnp.zeros((share, width), F32)
    for source in range(owners):
        scale = jnp.exp(of(peaks, source) - top)
        output = output + scale * landed[source][:, :width].astype(F32)
        total = total + scale * of(totals, source)
    attended = (output / total).astype(BF16)
    projected = jnp.dot(attended, w_out[...], preferred_element_type=F32)
    mean_sq = jnp.mean(projected * projected, axis=-1, keepdims=True)
    normed = projected * lax.rsqrt(mean_sq + 1e-06)
    latent_out[...] = (normed * out_gain[...]).astype(BF16)
    store = pltpu.make_async_copy(latent_out, latents, sem.at[1])
    store.start()
    move.wait()
    store.wait()


def per_device(
    n_sn,
    owners,
    point_features,
    point_positions,
    sn_positions,
    latent_queries,
    target_block,
    target_links,
    target_count,
    block_slot,
    w_in,
    w_mid,
    w_post,
    w_key,
    w_value,
    w_out,
    out_gain,
):
    targets = target_links.shape[0]
    width = point_features.shape[1]
    sn_rows = sn_positions.shape[1]
    sn_blocks = sn_rows // BLOCK
    latents = latent_queries.shape[0]
    share = latents // owners
    vmem = pl.BlockSpec(memory_space=pltpu.VMEM)
    hbm = pl.BlockSpec(memory_space=pl.ANY)
    dma = pltpu.SemaphoreType.DMA
    points = point_features.shape[0]
    rows_a = width // 2 + STAT_ROWS
    features_t, landed = pl.pallas_call(
        functools.partial(encoder_kernel, owners, n_sn, sn_blocks, targets),
        out_shape=(
            jax.ShapeDtypeStruct((width, sn_rows), BF16),
            jax.ShapeDtypeStruct((owners // n_sn, share, OUT_LANES), BF16),
        ),
        in_specs=[hbm] * 13,
        out_specs=(hbm, hbm),
        scratch_shapes=[
            pltpu.SMEM(target_block.shape, jnp.int32),
            pltpu.SMEM(target_links.shape[::-1], jnp.int32),
            pltpu.SMEM(target_count.shape, jnp.int32),
            pltpu.SMEM(block_slot.shape, jnp.int32),
            pltpu.VMEM((width, points), BF16),
            pltpu.VMEM(point_positions.shape, F32),
            pltpu.VMEM(sn_positions.shape, F32),
            pltpu.VMEM(w_in.shape, BF16),
            pltpu.VMEM(w_mid.shape, BF16),
            pltpu.VMEM(w_post.shape, BF16),
            pltpu.VMEM(latent_queries.shape[::-1], BF16),
            pltpu.VMEM(w_key.shape, BF16),
            pltpu.VMEM(w_value.shape, BF16),
            dma((13,)),
            pltpu.VMEM((width, sn_rows // 2), BF16),
            pltpu.VMEM((2, width, sn_rows // 2), BF16),
            pltpu.VMEM((width, sn_rows // 2), BF16),
            pltpu.VMEM((sn_rows // 2, width), BF16),
            pltpu.VMEM((HEADS, width, latents), BF16),
            pltpu.VMEM((HEADS, latents), F32),
            pltpu.VMEM((HEADS, latents), F32),
            pltpu.VMEM((width, latents), F32),
            pltpu.VMEM((HEADS, sn_rows // 2, latents), F32),
            pltpu.VMEM((HEADS, sn_rows // 2, latents), BF16),
            pltpu.VMEM((width, sn_rows), BF16),
            pltpu.VMEM((owners // n_sn, share, OUT_LANES), BF16),
            dma((owners // n_sn,)),
            dma((owners // n_sn,)),
            pltpu.VMEM((2, width + 8, latents // (2 * n_sn)), F32),
            pltpu.VMEM((2, width + 8, latents // (2 * n_sn)), F32),
            dma((2,)),
            dma((2,)),
            pltpu.VMEM((owners, rows_a, BLOCK), BF16),
            pltpu.VMEM((owners, width // 2, BLOCK), BF16),
            pltpu.VMEM((sn_blocks, rows_a, BLOCK), F32),
            pltpu.VMEM((sn_blocks, width // 2, BLOCK), F32),
            pltpu.SMEM((owners,), jnp.int32),
            pltpu.VMEM((owners, 3, BLOCK), F32),
            pltpu.VMEM((owners, 3, BLOCK), F32),
            pltpu.VMEM((points // BLOCK, width, BLOCK), BF16),
            pltpu.VMEM((points // BLOCK, 3, BLOCK), F32),
            pltpu.VMEM((owners, rows_a, BLOCK), BF16),
            pltpu.VMEM((owners, width // 2, BLOCK), BF16),
            pltpu.SMEM((targets,), jnp.int32),
            dma((owners,)),
            dma((owners,)),
            dma((owners,)),
            dma((owners,)),
            dma((owners,)),
            dma((owners,)),
            dma((3,)),
        ],
        compiler_params=pltpu.CompilerParams(
            collective_id=0, has_side_effects=True, vmem_limit_bytes=VMEM_LIMIT
        ),
        name="encoder",
    )(
        *(
            pltpu.with_memory_space_constraint(operand, pltpu.HBM)
            for operand in (
                target_block,
                target_links.T,
                target_count,
                block_slot,
                point_features.T,
                point_positions,
                sn_positions,
                w_in,
                w_mid,
                w_post,
                latent_queries.T,
                w_key,
                w_value,
            )
        )
    )
    features_t, latent_out = pl.pallas_call(
        finish_kernel,
        out_shape=(
            jax.ShapeDtypeStruct((width, sn_rows), BF16),
            jax.ShapeDtypeStruct((share, width), BF16),
        ),
        in_specs=[hbm] + [vmem] * 3,
        out_specs=(hbm, hbm),
        scratch_shapes=[pltpu.VMEM((share, width), BF16), dma((2,))],
        compiler_params=pltpu.CompilerParams(vmem_limit_bytes=VMEM_LIMIT),
        name="finish",
    )(features_t, landed, w_out, out_gain.reshape(1, width))
    return (features_t.T, latent_out)


def solution(mesh):
    n_sn = mesh.shape["sn"]
    owners = mesh.shape["pts"] * n_sn
    everything = ("groups", "pts", "sn")
    in_specs = (
        P(everything, None),
        P(None, everything),
        P(None, everything),
        P(),
        P("groups"),
        P(everything, None),
        P("groups"),
        P("groups"),
        P(),
        P(),
        P(),
        P(),
        P(),
        P(),
        P(),
    )
    out_specs = (P(everything, None), P(everything, None))
    return jax.shard_map(
        functools.partial(per_device, n_sn, owners),
        mesh=mesh,
        in_specs=in_specs,
        out_specs=out_specs,
        check_vma=False,
    )
```

```python
import functools

import jax
import jax.numpy as jnp
from jax import lax
from jax.experimental import pallas as pl
from jax.experimental.pallas import tpu as pltpu
from jax.sharding import PartitionSpec as P

HEADS = 3
BLOCK = 128
INV_RADIUS_SQ = 100.0
MESH = pl.DeviceIdType.MESH
STAT_ROWS = 8
CHUNK = 2048
OUT_LANES = 256
VMEM_LIMIT = 40 * 2**20
F32 = jnp.float32
BF16 = jnp.bfloat16


def contract(a, b, dim_a, dim_b):
    return lax.dot_general(a, b, (((dim_a,), (dim_b,)), ((), ())), preferred_element_type=F32)


def place(n_sn):
    return lax.axis_index("pts") * n_sn + lax.axis_index("sn")


def peer(index, n_sn):
    return {"pts": lax.div(index, n_sn), "sn": lax.rem(index, n_sn)}


def greet(owners, me, n_sn):
    barrier = pltpu.get_barrier_semaphore()

    def signal(i, carry):
        other = across_first(me, i, owners)
        pl.semaphore_signal(barrier, inc=1, device_id=peer(other, n_sn), device_id_type=MESH)
        return carry

    lax.fori_loop(0, owners - 1, signal, 0, unroll=owners <= 16)
    return barrier


def early_steps(steps):
    left = 3 - lax.div(lax.axis_index("pts") * 4, lax.axis_size("pts"))
    return steps // 2 * lax.div(left * left, 4)


def across_first(me, i, owners):
    left = owners - 1 - i
    top = 1
    bit = 2
    while bit < owners:
        top = jnp.where(left >= bit, bit, top)
        bit *= 2
    offset = 3 * top - 1 - left
    other = 0
    bit = 1
    while bit < owners:
        other = other + bit * lax.rem(lax.div(me, bit) + lax.div(offset, bit), 2)
        bit *= 2
    return other


def named_block(owner, targets, sn_blocks, count, slot_at):
    def look(k, state):
        which, block, live = state
        slot = slot_at(k)
        hit = jnp.logical_and(lax.div(slot, sn_blocks) == owner, k < count)
        return (
            jnp.where(hit, k, which),
            jnp.where(hit, lax.rem(slot, sn_blocks), block),
            jnp.where(hit, 1.0, live),
        )

    start = (jnp.int32(0), jnp.int32(0), F32(0.0))
    return lax.fori_loop(0, targets, look, start, unroll=targets <= 8)


def low_lanes(shape):
    return lax.broadcasted_iota(jnp.int32, shape, 1) < BLOCK // 2


def swap_halves(upper, lower):
    low = low_lanes(upper.shape)
    half = BLOCK // 2
    return (
        jnp.where(low, upper, pltpu.roll(lower, half, 1)),
        jnp.where(low, pltpu.roll(upper, half, 1), lower),
    )


def columns_of(rows):
    padded = jnp.concatenate([rows, jnp.zeros((5, rows.shape[1]), F32)], axis=0)
    return jnp.transpose(padded)


def thirds(x):
    first = x.astype(BF16).astype(F32)
    second = (x - first).astype(BF16).astype(F32)
    third = x - first - second
    return [first, second, third]


def encoder_kernel(
    owners,
    n_sn,
    sn_blocks,
    targets,
    target_block_in,
    target_links_in,
    target_count_in,
    block_slot_in,
    feats_in,
    positions_in,
    sn_positions_in,
    w_in_in,
    w_mid_in,
    w_post_in,
    queries_in,
    w_key_in,
    w_value_in,
    features_out,
    landed,
    target_block,
    target_links,
    target_count,
    block_slot,
    points,
    positions,
    sn_positions,
    w_in,
    w_mid,
    w_post,
    queries,
    w_key,
    w_value,
    load_sem,
    pooled,
    features,
    values_t,
    keys,
    masked,
    peak_so_far,
    total_so_far,
    out_so_far,
    all_scores,
    all_probs,
    w_post_t,
    w_value_t,
    whole_features,
    parts,
    part_send,
    part_recv,
    pair_out,
    pair_in,
    pair_send,
    pair_recv,
    arrived_a,
    arrived_b,
    sums_a,
    sums_b,
    block_of,
    wanted,
    everywhere,
    hidden,
    point_blocks,
    outgoing_a,
    outgoing_b,
    slots,
    pos_send,
    pos_recv,
    msg_send_a,
    msg_recv_a,
    msg_send_b,
    msg_recv_b,
    own_sem,
):
    me = place(n_sn)
    links = target_links.shape[0]
    width = points.shape[0]
    loads = [
        pltpu.make_async_copy(source, target, load_sem.at[i])
        for i, (source, target) in enumerate(
            [
                (target_block_in, target_block),
                (block_slot_in, block_slot),
                (target_count_in, target_count),
                (target_links_in, target_links),
                (sn_positions_in, sn_positions),
                (feats_in, points),
                (w_in_in, w_in),
                (w_mid_in, w_mid),
                (positions_in, positions),
                (w_post_in, w_post),
                (w_key_in, w_key),
                (w_value_in, w_value),
                (queries_in, queries),
            ]
        )
    ]
    for load in loads[:5]:
        load.start()
    barrier = greet(owners, me, n_sn)
    for load in loads[5:]:
        load.start()
    for load in loads[:5]:
        load.wait()

    def choose(region, carry):
        def slot_at(k):
            return block_slot[target_block[region * targets + k]]

        block = named_block(me, targets, sn_blocks, target_count[region], slot_at)[1]
        block_of[region] = block
        rows = sn_positions[:, :BLOCK]
        for b in range(1, sn_blocks):
            rows = jnp.where(block == b, sn_positions[:, b * BLOCK : (b + 1) * BLOCK], rows)
        wanted[region] = rows
        return carry

    lax.fori_loop(0, owners, choose, 0, unroll=4)

    def slot_of(k, carry):
        slots[k] = block_slot[target_block[me * targets + k]]
        return carry

    lax.fori_loop(0, targets, slot_of, 0)
    my_count = target_count[me]

    def pos_copy(other, slot_at):
        return pltpu.make_async_remote_copy(
            src_ref=wanted.at[other],
            dst_ref=everywhere.at[slot_at],
            send_sem=pos_send.at[other],
            recv_sem=pos_recv.at[slot_at],
            device_id=peer(other, n_sn),
            device_id_type=MESH,
        )

    def start_pos(i, carry):
        pos_copy(across_first(me, i, owners), me).start()
        return carry

    def mlp(step, carry):
        span = pl.ds(pl.multiple_of(step * CHUNK, CHUNK), CHUNK)
        inner = jax.nn.gelu(contract(w_in[...], points[:, span], 0, 0)).astype(BF16)
        hid = contract(w_mid[...], inner, 0, 0).astype(BF16)
        places = positions[:, span]
        for q in range(CHUNK // BLOCK):
            hidden[step * (CHUNK // BLOCK) + q] = hid[:, q * BLOCK : (q + 1) * BLOCK]
            point_blocks[step * (CHUNK // BLOCK) + q] = places[:, q * BLOCK : (q + 1) * BLOCK]
        return carry

    mlp_steps = points.shape[1] // CHUNK
    for load in loads[5:9]:
        load.wait()
    early = early_steps(mlp_steps)
    lax.fori_loop(0, early, mlp, 0)
    pl.semaphore_wait(barrier, owners - 1)
    lax.fori_loop(0, owners - 1, start_pos, 0, unroll=owners <= 16)
    own_pos = pltpu.make_async_copy(wanted.at[me], everywhere.at[me], own_sem.at[0])
    own_pos.start()
    lax.fori_loop(early, mlp_steps, mlp, 0)
    for load in loads[9:]:
        load.wait()

    outgoing = (outgoing_a, outgoing_b)
    arrived = (arrived_a, arrived_b)
    sums = (sums_a, sums_b)
    msg_send = (msg_send_a, msg_send_b)
    msg_recv = (msg_recv_a, msg_recv_b)
    half_rows = width // 2

    def msg_copy(p, other, slot_at):
        return pltpu.make_async_remote_copy(
            src_ref=outgoing[p].at[other],
            dst_ref=arrived[p].at[slot_at],
            send_sem=msg_send[p].at[other],
            recv_sem=msg_recv[p].at[slot_at],
            device_id=peer(other, n_sn),
            device_id_type=MESH,
        )

    def build(other):
        which, block, live = named_block(
            other, targets, sn_blocks, my_count, lambda k: slots[k]
        )
        sn_cols = columns_of(everywhere[other])
        kernels = []
        blocks = []
        for j in range(links):
            link = target_links[j, which]
            pts = point_blocks[link]
            dist = jnp.zeros((BLOCK, BLOCK), F32)
            for c in range(3):
                gap = sn_cols[:, c : c + 1] - pts[c : c + 1, :]
                dist = dist + gap * gap
            kernels.append(1.0 / (1.0 + dist * INV_RADIUS_SQ))
            blocks.append(hidden[link])
        total = kernels[0]
        for extra in kernels[1:]:
            total = total + extra
        total = jnp.sum(jnp.transpose(total), axis=0, keepdims=True)
        message = contract(
            jnp.concatenate(blocks, axis=1),
            jnp.concatenate([one.astype(BF16) for one in kernels], axis=1),
            1,
            1,
        )
        message = message * live
        halves = swap_halves(message[:half_rows], message[half_rows:])
        return (
            halves[0].astype(BF16),
            halves[1].astype(BF16),
            jnp.broadcast_to(total * live, (STAT_ROWS, BLOCK)).astype(BF16),
        )

    def nth(i):
        return across_first(me, i, owners)

    def build_next(i, carry):
        other = nth(i)
        pos_copy(other, other).wait_recv()
        first_half, second_half, total = build(other)
        outgoing_a[other, :half_rows, :] = first_half
        outgoing_a[other, half_rows:, :] = total
        outgoing_b[other] = second_half
        msg_copy(0, other, me).start()
        return carry

    lax.fori_loop(0, owners - 1, build_next, 0)

    def send_second(i, carry):
        msg_copy(1, nth(i), me).start()
        return carry

    lax.fori_loop(0, owners - 1, send_second, 0)
    own_pos.wait()
    own_first, own_second, own_total = build(me)
    outgoing_a[me, :half_rows, :] = own_first
    outgoing_a[me, half_rows:, :] = own_total
    outgoing_b[me] = own_second

    def source_of(n):
        return lax.rem(me + n, owners)

    def gather(p):
        sums[p][...] = jnp.zeros(sums[p].shape, F32)

        def add(source, message):
            block = block_of[source]
            for b in range(sn_blocks):
                sums[p][b] += jnp.where(block == b, message, 0.0)

        add(me, outgoing[p][me].astype(F32))

        def arrive(n, carry):
            source = source_of(n)
            msg_copy(p, source, source).wait_recv()
            add(source, arrived[p][source].astype(F32))
            return carry

        lax.fori_loop(1, owners, arrive, 0)

    def pool(p):
        for pair in range(sn_blocks // 2):
            scaled = []
            for b in (2 * pair, 2 * pair + 1):
                total = sums_a[b][half_rows : half_rows + 1, :]
                scale = 1.0 / (1.0 + total)
                scale = swap_halves(scale, scale)[p]
                scaled.append(sums[p][b][:half_rows, :] * scale)
            upper, lower = swap_halves(scaled[0], scaled[1])
            columns = slice(pair * BLOCK, (pair + 1) * BLOCK)
            pooled[:half_rows, columns] = upper.astype(BF16)
            pooled[half_rows:, columns] = lower.astype(BF16)

    head_width = width // HEADS
    latents = queries.shape[1]
    share = latents // owners
    group = latents // 2
    piece = group // n_sn
    places = owners // n_sn
    my_pts = lax.axis_index("pts")
    my_sn = lax.axis_index("sn")
    row_head = lax.broadcasted_iota(jnp.int32, queries.shape, 0) // head_width
    column = lax.broadcasted_iota(jnp.int32, (latents, latents), 1)
    inside = column % piece
    place_of = column // group * (places // 2) + inside // share
    taken = (place_of * n_sn + column % group // piece) * share + inside % share
    pick = lax.broadcasted_iota(jnp.int32, (latents, latents), 0) == taken
    by_core = contract(queries[...], jnp.where(pick, 1.0, 0.0).astype(BF16), 1, 0).astype(BF16)
    scaled_queries = by_core * BF16(head_width ** (-0.5))
    for h in range(HEADS):
        masked[h] = jnp.where(row_head == h, scaled_queries, BF16(0.0))

    spot = lax.broadcasted_iota(jnp.int32, w_post.shape, 0)
    unit = jnp.where(spot == lax.broadcasted_iota(jnp.int32, w_post.shape, 1), 1.0, 0.0)
    w_post_t[...] = contract(w_post[...], unit.astype(BF16), 0, 0).astype(BF16)
    w_value_t[...] = contract(w_value[...], unit.astype(BF16), 0, 0).astype(BF16)

    def project(p):
        pool(p)
        features[p] = jax.nn.gelu(contract(w_post_t[...], pooled[...], 1, 0)).astype(BF16)
        keys[...] = contract(features[p], w_key[...], 0, 0).astype(BF16)
        values_t[...] = contract(w_value_t[...], features[p], 1, 0).astype(BF16)

    def head_rows(h):
        return slice(h * head_width, (h + 1) * head_width)

    def score():
        for side in range(2):
            lanes = slice(side * group, (side + 1) * group)
            for h in range(HEADS):
                all_scores[h, :, lanes] = contract(keys[...], masked[h, :, lanes], 1, 0)

    def weigh(h, lanes):
        return contract(values_t[head_rows(h), :], all_probs[h, :, lanes], 1, 0)

    gather(0)
    project(0)
    score()
    for h in range(HEADS):
        for at in range(0, latents, piece):
            lanes = slice(at, at + piece)
            scores = all_scores[h, :, lanes]
            peak = jnp.max(scores, axis=0, keepdims=True)
            probs = jnp.exp(scores - peak)
            peak_so_far[h : h + 1, lanes] = peak
            total_so_far[h : h + 1, lanes] = jnp.sum(probs, axis=0, keepdims=True)
            all_probs[h, :, lanes] = probs.astype(BF16)
    for side in range(2):
        lanes = slice(side * group, (side + 1) * group)
        for h in range(HEADS):
            out_so_far[head_rows(h), lanes] = weigh(h, lanes)
    def sent_first(i, carry):
        msg_copy(0, nth(i), nth(i)).wait_send()
        pos_copy(nth(i), nth(i)).wait_send()
        return carry

    lax.fori_loop(0, owners - 1, sent_first, 0)
    gather(1)
    project(1)

    def attend(side, core):
        lanes = pl.ds(pl.multiple_of(side * group + core * piece, piece), piece)
        kept = []
        for h in range(HEADS):
            scores = all_scores[h, :, lanes]
            old_peak = peak_so_far[h : h + 1, lanes]
            peak = jnp.maximum(old_peak, jnp.max(scores, axis=0, keepdims=True))
            shrink = jnp.exp(old_peak - peak)
            probs = jnp.exp(scores - peak)
            total = jnp.sum(probs, axis=0, keepdims=True)
            all_probs[h, :, lanes] = probs.astype(BF16)
            kept.append((peak, total + shrink * total_so_far[h : h + 1, lanes], shrink))
        state = []
        for h, (peak, total, shrink) in enumerate(kept):
            out = weigh(h, lanes) + shrink * out_so_far[head_rows(h), lanes]
            state.append((peak, total, out))
        return state

    def pair_copy(side):
        return pltpu.make_async_remote_copy(
            src_ref=pair_out.at[side],
            dst_ref=pair_in.at[side],
            send_sem=pair_send.at[side],
            recv_sem=pair_recv.at[side],
            device_id={"pts": my_pts, "sn": 1 - my_sn},
            device_id_type=MESH,
        )

    def copy_of(other, slot_at):
        return pltpu.make_async_remote_copy(
            src_ref=parts.at[other],
            dst_ref=landed.at[slot_at],
            send_sem=part_send.at[other],
            recv_sem=part_recv.at[slot_at],
            device_id={"pts": other, "sn": my_sn},
            device_id_type=MESH,
        )

    def hand_over(side):
        for h, (peak, total, out) in enumerate(attend(side, 1 - my_sn)):
            pair_out[side, head_rows(h), :] = out
            pair_out[side, width + h : width + h + 1, :] = peak
            pair_out[side, width + HEADS + h : width + HEADS + h + 1, :] = total
        pair_out[side, width + 2 * HEADS :, :] = jnp.zeros((8 - 2 * HEADS, piece), F32)
        pair_copy(side).start()

    def merge(side, mine):
        pair_copy(side).wait_recv()
        outs, peaks, totals = [], [], []
        for h, (peak, total, out) in enumerate(mine):
            their_peak = pair_in[side, width + h : width + h + 1, :]
            their_total = pair_in[side, width + HEADS + h : width + HEADS + h + 1, :]
            top = jnp.maximum(peak, their_peak)
            shrink = jnp.exp(peak - top)
            their_shrink = jnp.exp(their_peak - top)
            peaks += thirds(top)
            totals += thirds(total * shrink + their_total * their_shrink)
            outs.append(out * shrink + pair_in[side, head_rows(h), :] * their_shrink)
        pad = jnp.zeros((OUT_LANES - width - 6 * HEADS, piece), F32)
        merged = jnp.concatenate(outs + peaks + totals + [pad], axis=0)
        merged = jnp.transpose(merged.astype(BF16))
        first_place = side * (places // 2)
        for j in range(places // 2):
            parts[first_place + j] = merged[j * share : (j + 1) * share, :]

        def send_part(j, carry):
            other = first_place + j

            @pl.when(other != my_pts)
            def _():
                copy_of(other, my_pts).start()

            return carry

        lax.fori_loop(0, places // 2, send_part, 0, unroll=places <= 8)

    score()
    hand_over(0)
    near = attend(0, my_sn)
    hand_over(1)
    merge(0, near)
    merge(1, attend(1, my_sn))
    own = pltpu.make_async_copy(parts.at[my_pts], landed.at[my_pts], own_sem.at[1])
    own.start()
    for pair in range(sn_blocks // 2):
        columns = slice(pair * BLOCK, (pair + 1) * BLOCK)
        whole = swap_halves(features[0, :, columns].astype(F32), features[1, :, columns].astype(F32))
        for side in range(2):
            at = (2 * pair + side) * BLOCK
            whole_features[:, at : at + BLOCK] = whole[side].astype(BF16)
    store = pltpu.make_async_copy(whole_features, features_out, own_sem.at[2])
    store.start()

    def sent(i, carry):
        msg_copy(1, nth(i), nth(i)).wait_send()
        return carry

    lax.fori_loop(0, owners - 1, sent, 0)
    pair_copy(0).wait_send()
    pair_copy(1).wait_send()
    own.wait()

    def settle(off, carry):
        other = lax.rem(my_pts + off, places)
        copy = copy_of(other, other)
        copy.wait_send()
        copy.wait_recv()
        return carry

    lax.fori_loop(1, places, settle, 0)
    store.wait()


def finish_kernel(features_in, landed, w_out, out_gain, features, latents, latent_out, sem):
    move = pltpu.make_async_copy(features_in, features, sem.at[0])
    move.start()
    owners, share, _ = landed.shape
    width = w_out.shape[0]
    head_width = width // HEADS
    lane = lax.broadcasted_iota(jnp.int32, (OUT_LANES, width), 0) - width
    head_of = lax.broadcasted_iota(jnp.int32, (OUT_LANES, width), 1) // head_width
    is_peak = jnp.logical_and(lane >= 3 * head_of, lane < 3 * head_of + 3)
    total_lane = lane - 3 * HEADS
    is_total = jnp.logical_and(total_lane >= 3 * head_of, total_lane < 3 * head_of + 3)
    flat = jnp.concatenate([landed[source] for source in range(owners)], axis=0)
    peaks = contract(flat, jnp.where(is_peak, 1.0, 0.0).astype(BF16), 1, 0)
    totals = contract(flat, jnp.where(is_total, 1.0, 0.0).astype(BF16), 1, 0)

    def of(full, source):
        return full[source * share : (source + 1) * share, :]

    top = of(peaks, 0)
    for source in range(1, owners):
        top = jnp.maximum(top, of(peaks, source))
    output = jnp.zeros((share, width), F32)
    total = jnp.zeros((share, width), F32)
    for source in range(owners):
        scale = jnp.exp(of(peaks, source) - top)
        output = output + scale * landed[source][:, :width].astype(F32)
        total = total + scale * of(totals, source)
    attended = (output / total).astype(BF16)
    projected = jnp.dot(attended, w_out[...], preferred_element_type=F32)
    mean_sq = jnp.mean(projected * projected, axis=-1, keepdims=True)
    normed = projected * lax.rsqrt(mean_sq + 1e-06)
    latent_out[...] = (normed * out_gain[...]).astype(BF16)
    store = pltpu.make_async_copy(latent_out, latents, sem.at[1])
    store.start()
    move.wait()
    store.wait()


def per_device(
    n_sn,
    owners,
    point_features,
    point_positions,
    sn_positions,
    latent_queries,
    target_block,
    target_links,
    target_count,
    block_slot,
    w_in,
    w_mid,
    w_post,
    w_key,
    w_value,
    w_out,
    out_gain,
):
    targets = target_links.shape[0]
    width = point_features.shape[1]
    sn_rows = sn_positions.shape[1]
    sn_blocks = sn_rows // BLOCK
    latents = latent_queries.shape[0]
    share = latents // owners
    vmem = pl.BlockSpec(memory_space=pltpu.VMEM)
    hbm = pl.BlockSpec(memory_space=pl.ANY)
    dma = pltpu.SemaphoreType.DMA
    points = point_features.shape[0]
    rows_a = width // 2 + STAT_ROWS
    features_t, landed = pl.pallas_call(
        functools.partial(encoder_kernel, owners, n_sn, sn_blocks, targets),
        out_shape=(
            jax.ShapeDtypeStruct((width, sn_rows), BF16),
            jax.ShapeDtypeStruct((owners // n_sn, share, OUT_LANES), BF16),
        ),
        in_specs=[hbm] * 13,
        out_specs=(hbm, hbm),
        scratch_shapes=[
            pltpu.SMEM(target_block.shape, jnp.int32),
            pltpu.SMEM(target_links.shape[::-1], jnp.int32),
            pltpu.SMEM(target_count.shape, jnp.int32),
            pltpu.SMEM(block_slot.shape, jnp.int32),
            pltpu.VMEM((width, points), BF16),
            pltpu.VMEM(point_positions.shape, F32),
            pltpu.VMEM(sn_positions.shape, F32),
            pltpu.VMEM(w_in.shape, BF16),
            pltpu.VMEM(w_mid.shape, BF16),
            pltpu.VMEM(w_post.shape, BF16),
            pltpu.VMEM(latent_queries.shape[::-1], BF16),
            pltpu.VMEM(w_key.shape, BF16),
            pltpu.VMEM(w_value.shape, BF16),
            dma((13,)),
            pltpu.VMEM((width, sn_rows // 2), BF16),
            pltpu.VMEM((2, width, sn_rows // 2), BF16),
            pltpu.VMEM((width, sn_rows // 2), BF16),
            pltpu.VMEM((sn_rows // 2, width), BF16),
            pltpu.VMEM((HEADS, width, latents), BF16),
            pltpu.VMEM((HEADS, latents), F32),
            pltpu.VMEM((HEADS, latents), F32),
            pltpu.VMEM((width, latents), F32),
            pltpu.VMEM((HEADS, sn_rows // 2, latents), F32),
            pltpu.VMEM((HEADS, sn_rows // 2, latents), BF16),
            pltpu.VMEM(w_post.shape, BF16),
            pltpu.VMEM(w_value.shape, BF16),
            pltpu.VMEM((width, sn_rows), BF16),
            pltpu.VMEM((owners // n_sn, share, OUT_LANES), BF16),
            dma((owners // n_sn,)),
            dma((owners // n_sn,)),
            pltpu.VMEM((2, width + 8, latents // (2 * n_sn)), F32),
            pltpu.VMEM((2, width + 8, latents // (2 * n_sn)), F32),
            dma((2,)),
            dma((2,)),
            pltpu.VMEM((owners, rows_a, BLOCK), BF16),
            pltpu.VMEM((owners, width // 2, BLOCK), BF16),
            pltpu.VMEM((sn_blocks, rows_a, BLOCK), F32),
            pltpu.VMEM((sn_blocks, width // 2, BLOCK), F32),
            pltpu.SMEM((owners,), jnp.int32),
            pltpu.VMEM((owners, 3, BLOCK), F32),
            pltpu.VMEM((owners, 3, BLOCK), F32),
            pltpu.VMEM((points // BLOCK, width, BLOCK), BF16),
            pltpu.VMEM((points // BLOCK, 3, BLOCK), F32),
            pltpu.VMEM((owners, rows_a, BLOCK), BF16),
            pltpu.VMEM((owners, width // 2, BLOCK), BF16),
            pltpu.SMEM((targets,), jnp.int32),
            dma((owners,)),
            dma((owners,)),
            dma((owners,)),
            dma((owners,)),
            dma((owners,)),
            dma((owners,)),
            dma((3,)),
        ],
        compiler_params=pltpu.CompilerParams(
            collective_id=0, has_side_effects=True, vmem_limit_bytes=VMEM_LIMIT
        ),
        name="encoder",
    )(
        *(
            pltpu.with_memory_space_constraint(operand, pltpu.HBM)
            for operand in (
                target_block,
                target_links.T,
                target_count,
                block_slot,
                point_features.T,
                point_positions,
                sn_positions,
                w_in,
                w_mid,
                w_post,
                latent_queries.T,
                w_key,
                w_value,
            )
        )
    )
    features_t, latent_out = pl.pallas_call(
        finish_kernel,
        out_shape=(
            jax.ShapeDtypeStruct((width, sn_rows), BF16),
            jax.ShapeDtypeStruct((share, width), BF16),
        ),
        in_specs=[hbm] + [vmem] * 3,
        out_specs=(hbm, hbm),
        scratch_shapes=[pltpu.VMEM((share, width), BF16), dma((2,))],
        compiler_params=pltpu.CompilerParams(vmem_limit_bytes=VMEM_LIMIT),
        name="finish",
    )(features_t, landed, w_out, out_gain.reshape(1, width))
    return (features_t.T, latent_out)


def solution(mesh):
    n_sn = mesh.shape["sn"]
    owners = mesh.shape["pts"] * n_sn
    everything = ("groups", "pts", "sn")
    in_specs = (
        P(everything, None),
        P(None, everything),
        P(None, everything),
        P(),
        P("groups"),
        P(everything, None),
        P("groups"),
        P("groups"),
        P(),
        P(),
        P(),
        P(),
        P(),
        P(),
        P(),
    )
    out_specs = (P(everything, None), P(everything, None))
    return jax.shard_map(
        functools.partial(per_device, n_sn, owners),
        mesh=mesh,
        in_specs=in_specs,
        out_specs=out_specs,
        check_vma=False,
    )
```
